256 devices in a mesh: sec: 8 (over y, core), tile: 32 (over z, x).
Axes of the slice: x: 4, y: 4, z: 8, core: 2. Of those that a mesh axis runs over, the one named last changes fastest.
Arguments:
- tile_strips: bfloat16 [8, 32, 2, 5, 64, 512], P('sec', 'tile'), may hold values from -6 to 6, as said below
- pair_mask: int32 [8, 32, 2, 3], P('sec', 'tile'), may hold values 0 or 1
- strip_offset: int32 [8, 32, 2, 3, 2], P('sec', 'tile'), may hold values from -16 to 16
- stiffness: float32 [8, 32, 2], P('sec', 'tile'), may hold values from 0.05 to 0.5
Outputs:
- affine_update: float32 [6, 8, 32, 2], P(None, 'sec', 'tile')
- residual: float32 [6, 8, 32, 2], P(None, 'sec', 'tile')
The draws below stay inside these ranges and needn't reach their ends.
Inputs may be any that keep to these rules, and one draw needn't show every extreme that they name: `tile_strips`: neighbouring tiles' intersecting images are correlated.
All inputs are finite; a program needn't handle non-finite values. No bound on the sum of `pair_mask` on one device may be relied on, other than what follows from the above.
Results may differ from the reference program's by a relative error of at most 0.0013.
Values may be sent and summed in bfloat16 or wider, within the bound.
No kernel may reach another device: no remote copies, remote signals or barrier semaphores. Data moves between devices by JAX's collectives and lax.ppermute only.
A program may use at most 64 MiB of HBM per device.

```python
import math
import jax
import jax.numpy as jnp
from jax import lax

GRID_C = 2
STRIP_H = 64
STRIP_W = 512
ITERS = 3
SECTIONS = 8
GRID_R = 32


def draw_tile_strips(key, part):
    keys = jax.random.split(key, 7)
    full = (SECTIONS, GRID_R, GRID_C, STRIP_H, STRIP_W)
    own_right = jax.random.normal(keys[0], full, jnp.float32)
    own_bottom = jax.random.normal(keys[1], full, jnp.float32)
    patches = jax.random.normal(keys[2], full, jnp.float32)
    first_left = jax.random.normal(keys[3], (SECTIONS, GRID_R, 1, STRIP_H, STRIP_W), jnp.float32)
    fresh_left = jax.random.normal(keys[4], (SECTIONS, GRID_R, GRID_C - 1, STRIP_H, STRIP_W), jnp.float32)
    first_top = jax.random.normal(keys[5], (SECTIONS, 1, GRID_C, STRIP_H, STRIP_W), jnp.float32)
    fresh_top = jax.random.normal(keys[6], (SECTIONS, GRID_R - 1, GRID_C, STRIP_H, STRIP_W), jnp.float32)
    left = jnp.concatenate([first_left, 0.8 * jnp.roll(own_right, 1, axis=4)[:, :, :-1] + 0.6 * fresh_left], axis=2)
    top = jnp.concatenate([first_top, 0.8 * jnp.roll(own_bottom, 1, axis=3)[:, :-1] + 0.6 * fresh_top], axis=1)
    chain = [patches[0]]
    for index in range(1, SECTIONS):
        chain.append(0.8 * jnp.roll(chain[-1], 1, axis=3) + 0.6 * patches[index])
    patch = jnp.stack(chain)
    strips = jnp.stack([left, own_right, top, own_bottom, patch], axis=3)
    return jnp.clip(strips, -6.0, 6.0).astype(jnp.bfloat16)


def place_ends(entries, own_key, least, top_value):
    longest = entries.shape.index(max(entries.shape))
    spots = []
    for shift in (0, 1):
        where = [jax.random.randint(jax.random.fold_in(own_key, axis), (), 0, length) for axis, length in enumerate(entries.shape)]
        where[longest] = (where[longest] + shift) % entries.shape[longest]
        spots.append(tuple(where))
    return entries.at[spots[0]].set(least).at[spots[1]].set(top_value)


def steps_of(rng, extent, shards, smallest, high):
    level = 1.0
    for position, blocks in shards:
        heights = jax.random.uniform(jax.random.fold_in(jax.random.fold_in(rng, 6), position), (blocks,), jnp.float32, smallest / len(shards), high / len(shards))
        level = level * jnp.repeat(jnp.exp(heights), extent[position] // blocks).reshape((-1,) + (1,) * (len(extent) - 1 - position))
    return level


def setup_inputs(seed: int = 0) -> dict:
    key_list = jax.random.split(jax.random.key(seed), 5)
    return {
        "tile_strips": draw_tile_strips(jax.random.fold_in(key_list[4], 71), 0),
        "pair_mask": place_ends((jax.random.randint(key_list[1], (SECTIONS, GRID_R, GRID_C, 3), 0, 5) < 4).astype(jnp.int32), jax.random.fold_in(key_list[1], 1), 0, 1),
        "strip_offset": place_ends(jax.random.randint(key_list[2], (SECTIONS, GRID_R, GRID_C, 3, 2), -(STRIP_H // 4), STRIP_H // 4 + 1), jax.random.fold_in(key_list[2], 1), -(STRIP_H // 4), (STRIP_H // 4 + 1) - 1).astype(jnp.int32),
        "stiffness": jnp.clip(jnp.exp(math.log(0.5) - 2.3025851 * jax.random.uniform(key_list[3], (SECTIONS, GRID_R, GRID_C), jnp.float32) ** steps_of(key_list[3], (SECTIONS, GRID_R, GRID_C), ((0, 8), (1, 32)), -0.2, 0.2)), 0.05, 0.5),
    }


highest = lax.Precision.HIGHEST

def strip_gradients(image):
    padded = jnp.pad(image, 1)
    along_x = (padded[1:-1, 2:] - padded[1:-1, :-2]) * 0.5
    along_y = (padded[2:, 1:-1] - padded[:-2, 1:-1]) * 0.5
    return (along_x, along_y)

def jacobian_rows(image, shift_x, shift_y):
    height, width = image.shape
    column_grid = jnp.arange(width, dtype=jnp.float32)[None, :]
    row_grid = jnp.arange(height, dtype=jnp.float32)[:, None]
    coord_u = (column_grid + shift_x) / width - 0.5
    coord_v = (row_grid + shift_y) / height - 0.5
    along_x, along_y = strip_gradients(image)
    stacked = jnp.stack([along_x * coord_u, along_x * coord_v, along_x, along_y * coord_u, along_y * coord_v, along_y])
    return stacked.reshape(6, height * width)

def pair_block(image_a, image_b, offset):
    first = image_a.astype(jnp.float32)
    second = image_b.astype(jnp.float32)
    shifts = offset.astype(jnp.float32)
    zero = jnp.zeros((), jnp.float32)
    jacobian = jnp.concatenate([jacobian_rows(first, zero, zero), -jacobian_rows(second, shifts[0], shifts[1])], axis=0)
    pixels = first.shape[0] * first.shape[1]
    misfit = (first - second).reshape(pixels)
    normal = jnp.dot(jacobian, jacobian.T, precision=highest, preferred_element_type=jnp.float32) / pixels
    pull = -jnp.dot(jacobian, misfit, precision=highest, preferred_element_type=jnp.float32) / pixels
    return (normal, pull)

def to_next(array, axis):
    lead = jnp.zeros_like(lax.slice_in_dim(array, 0, 1, axis=axis))
    return jnp.concatenate([lead, lax.slice_in_dim(array, 0, array.shape[axis] - 1, axis=axis)], axis=axis)

def from_next(array, axis):
    tail = jnp.zeros_like(lax.slice_in_dim(array, 0, 1, axis=axis))
    return jnp.concatenate([lax.slice_in_dim(array, 1, array.shape[axis], axis=axis), tail], axis=axis)

def apply_block(block, vector):
    return jnp.einsum('ij...,j...->i...', block, vector, precision=highest)

def cholesky_rows(matrix):
    order = matrix.shape[0]
    factor = [[None] * order for index in range(order)]
    for column in range(order):
        pivot = matrix[column, column]
        for inner in range(column):
            pivot = pivot - factor[column][inner] * factor[column][inner]
        pivot = jnp.sqrt(pivot)
        factor[column][column] = pivot
        for row in range(column + 1, order):
            entry = matrix[row, column]
            for inner in range(column):
                entry = entry - factor[row][inner] * factor[column][inner]
            factor[row][column] = entry / pivot
    return factor

def solve_rows(factor, vector):
    order = len(factor)
    forward = []
    for row in range(order):
        value = vector[row]
        for inner in range(row):
            value = value - factor[row][inner] * forward[inner]
        forward.append(value / factor[row][row])
    backward = [None] * order
    for row in reversed(range(order)):
        value = forward[row]
        for inner in range(row + 1, order):
            value = value - factor[inner][row] * backward[inner]
        backward[row] = value / factor[row][row]
    return jnp.stack(backward)

def grid_blocks(images_a, images_b, offsets, exists):
    sections, tile_rows, columns, height, width = images_a.shape
    flat = (images_a.reshape(sections * tile_rows, columns, height, width), images_b.reshape(sections * tile_rows, columns, height, width), offsets.reshape(sections * tile_rows, columns, 2))
    normal, pull = lax.map(lambda items: jax.vmap(pair_block)(items[0], items[1], items[2]), flat)
    normal = normal.reshape(sections, tile_rows, columns, 12, 12).transpose(3, 4, 0, 1, 2) * exists
    pull = pull.reshape(sections, tile_rows, columns, 12).transpose(3, 0, 1, 2) * exists
    return (normal, pull)

def reference(tile_strips, pair_mask, strip_offset, stiffness):
    sections, tile_rows, columns = (tile_strips.shape[0], tile_strips.shape[1], tile_strips.shape[2])
    section_index = jnp.arange(sections)[:, None, None]
    row_index = jnp.arange(tile_rows)[None, :, None]
    column_index = jnp.arange(columns)[None, None, :]
    exists_right = ((pair_mask[..., 0] == 1) & (column_index < columns - 1)).astype(jnp.float32)
    exists_down = ((pair_mask[..., 1] == 1) & (row_index < tile_rows - 1)).astype(jnp.float32)
    exists_cross = ((pair_mask[..., 2] == 1) & (section_index < sections - 1)).astype(jnp.float32)
    normal_right, pull_right = grid_blocks(tile_strips[:, :, :, 1], from_next(tile_strips[:, :, :, 0], 2), strip_offset[:, :, :, 0], exists_right)
    normal_down, pull_down = grid_blocks(tile_strips[:, :, :, 3], from_next(tile_strips[:, :, :, 2], 1), strip_offset[:, :, :, 1], exists_down)
    normal_cross, pull_cross = grid_blocks(tile_strips[:, :, :, 4], from_next(tile_strips[:, :, :, 4], 0), strip_offset[:, :, :, 2], exists_cross)
    identity = jnp.eye(6, dtype=jnp.float32)[:, :, None, None, None]
    diagonal = stiffness[None, None] * identity + normal_right[:6, :6] + to_next(normal_right[6:, 6:], 4)
    diagonal = diagonal + normal_down[:6, :6] + to_next(normal_down[6:, 6:], 3)
    diagonal = diagonal + normal_cross[:6, :6] + to_next(normal_cross[6:, 6:], 2)
    load = pull_right[:6] + to_next(pull_right[6:], 3) + pull_down[:6] + to_next(pull_down[6:], 2)
    load = load + pull_cross[:6] + to_next(pull_cross[6:], 1)
    couplings = ((normal_right[:6, 6:], 3), (normal_down[:6, 6:], 2), (normal_cross[:6, 6:], 1))

    def multiply(vector):
        result = apply_block(diagonal, vector)
        for coupling, axis in couplings:
            result = result + apply_block(coupling, from_next(vector, axis))
            result = result + to_next(apply_block(jnp.swapaxes(coupling, 0, 1), vector), axis)
        return result
    factor = cholesky_rows(diagonal)
    affine_update = jnp.zeros_like(load)
    residual = load
    scaled = solve_rows(factor, residual)
    direction = scaled
    rho_now = jnp.sum(residual * scaled)
    for step in range(ITERS):
        product = multiply(direction)
        step_size = rho_now / jnp.sum(direction * product)
        affine_update = affine_update + step_size * direction
        residual = residual - step_size * product
        scaled = solve_rows(factor, residual)
        rho_next = jnp.sum(residual * scaled)
        direction = scaled + rho_next / rho_now * direction
        rho_now = rho_next
    return (affine_update, residual)
```

```python
import functools

import jax
import jax.numpy as jnp
from jax import lax
from jax.experimental import pallas as pl
from jax.experimental.pallas import tpu as pltpu
from jax.sharding import Mesh, PartitionSpec as P

ITERS = 3
H, W = 64, 512
F32 = jnp.float32
LANES = 128
SELF_H, SELF_T, SELF_B, SELF_P = 0, 3, 6, 9
CROSS = {"down": 12, "sec": 16}
CROSS_RIGHT = 20
PULL_RIGHT = 22
PULL = {"down": 24, "sec": 28}
META_LANE = 44
SCALE = 2.0**-17

VMEM = pl.BlockSpec(memory_space=pltpu.VMEM)
SMEM = pl.BlockSpec(memory_space=pltpu.SMEM)


def iota(shape, axis):
    return lax.broadcasted_iota(jnp.int32, shape, axis)


def store_gradients(image, gx_ref, gy_ref):
    col = iota((H, W), 1)
    row = iota((H, W), 0)
    ahead = jnp.where(col < W - 1, pltpu.roll(image, W - 1, 1), 0.0)
    behind = jnp.where(col > 0, pltpu.roll(image, 1, 1), 0.0)
    gx_ref[...] = ahead - behind
    below = jnp.where(row < H - 1, pltpu.roll(image, H - 1, 0), 0.0)
    above = jnp.where(row > 0, pltpu.roll(image, 1, 0), 0.0)
    gy_ref[...] = below - above


def row_moments(sums, level):
    s = iota((8, LANES), 0).astype(F32)
    c = 0.5 + s / H
    out = [sums[0], c * sums[0] - sums[1] * 0.125]
    if level == 3:
        out.append(c * c * sums[0] - (0.25 * c) * sums[1] + (2.0 * sums[2] - sums[1]) * (1.0 / 64.0))
    return out


def accumulate(fields, level):
    sums = None
    for k in range(8):
        values = fields(k)
        if sums is None:
            sums = [[v] * lv for v, lv in zip(values, level)]
            continue
        new = []
        for v, old, lv in zip(values, sums, level):
            now = [old[0] + v]
            for q in range(1, lv):
                now.append(old[q] + now[q - 1])
            new.append(now)
        sums = new
    return [row_moments(s, lv) for s, lv in zip(sums, level)]


def tree8(vs):
    s = iota((8, LANES), 0)
    m4 = s < 4
    w = []
    for i in range(4):
        x = jnp.where(m4, vs[i], vs[i + 4])
        y = jnp.where(m4, vs[i + 4], vs[i])
        w.append(x + pltpu.roll(y, 4, 0))
    m2 = (s & 2) == 0
    z = []
    for i in range(2):
        x = jnp.where(m2, w[i], w[i + 2])
        y = jnp.where(m2, w[i + 2], w[i])
        z.append(x + jnp.where(m2, pltpu.roll(y, 6, 0), pltpu.roll(y, 2, 0)))
    m1 = (s & 1) == 0
    x = jnp.where(m1, z[0], z[1])
    y = jnp.where(m1, z[1], z[0])
    return x + jnp.where(m1, pltpu.roll(y, 7, 0), pltpu.roll(y, 1, 0))


def put_group(group, lt, found, low_ref, high_ref):
    lanes = pl.ds(lt * LANES, LANES)
    order = [found[(f, t)] for f in range(4) for t in range(2)]
    for q in range(3):
        if not any(len(v) > q for v in order):
            continue
        vs = [v[q] if len(v) > q else jnp.zeros((8, LANES), F32) for v in order]
        total = tree8(vs)
        if q < 2:
            low_ref[pl.ds(64 * q + 8 * group, 8), lanes] = total
        else:
            high_ref[pl.ds(64 + 8 * group, 8), lanes] = total


def column_moments(low_ref, high_ref):
    r = iota((8, W), 0)
    u = iota((8, W), 1).astype(F32) / W - 0.5
    w = jnp.where(r == 0, 1.0, jnp.where(r == 1, u, u * u)) * SCALE
    dims = (((1,), (1,)), ((), ()))
    low = lax.dot_general(w, low_ref[...], dims, precision=lax.Precision.HIGHEST, preferred_element_type=F32)
    ones = jnp.full((8, W), SCALE, F32)
    high = lax.dot_general(ones, high_ref[...], dims, precision=lax.Precision.HIGHEST, preferred_element_type=F32)
    row = iota((8, LANES), 0)
    lane = iota((8, LANES), 1)
    return jnp.where((row == 2) & (lane >= 64), high, jnp.where(row < 3, low, 0.0))


def pair_fields(gxa, gya, gxb, gyb, misfit, lanes):
    def fields(k):
        rows = pl.ds(8 * k, 8)
        xa, ya, xb, yb, m = (ref[rows, lanes] for ref in (gxa, gya, gxb, gyb, misfit))
        return [xa * xb, xa * yb, ya * xb, ya * yb, xa * m, ya * m, xb * m, yb * m]

    return fields


def self_fields(gx, gy, lanes):
    def fields(k):
        rows = pl.ds(8 * k, 8)
        x, y = gx[rows, lanes], gy[rows, lanes]
        return [x * x, x * y, y * y]

    return fields


PAIR_LEVEL = (3, 3, 3, 3, 2, 2, 2, 2)


def cut_kernel(strips, tops, patches, sems):
    copies = []
    for t in range(2):
        copies.append(pltpu.make_async_copy(strips.at[0, 0, t, 2], tops.at[t], sems.at[t]))
        copies.append(pltpu.make_async_copy(strips.at[0, 0, t, 4], patches.at[t], sems.at[2 + t]))
    for copy in copies:
        copy.start()
    for copy in copies:
        copy.wait()


def own_kernel(strips, mask, offset, stiff, out, grad, misfit, low, high):
    low[...] = jnp.zeros_like(low)
    high[...] = jnp.zeros_like(high)
    kinds = ((1, 0), (2, 2), (3, 3), (4, 4))
    for kind, images in enumerate(kinds):
        for t in range(2):
            image = strips[0, 0, t, images[t]].astype(F32)
            store_gradients(image, grad.at[kind, t, 0], grad.at[kind, t, 1])
    misfit[...] = strips[0, 0, 0, 1].astype(F32) - strips[0, 0, 1, 0].astype(F32)
    for lt in range(4):
        lanes = pl.ds(lt * LANES, LANES)
        found = {}
        for kind in range(4):
            for t in range(2):
                got = accumulate(self_fields(grad.at[kind, t, 0], grad.at[kind, t, 1], lanes), (3, 3, 3))
                for n in range(3):
                    found[(3 * kind + n, t)] = got[n]
        for group in range(3):
            put_group(group, lt, {(f, t): found[(4 * group + f, t)] for f in range(4) for t in range(2)}, low, high)
        got = accumulate(
            pair_fields(grad.at[0, 0, 0], grad.at[0, 0, 1], grad.at[0, 1, 0], grad.at[0, 1, 1], misfit, lanes),
            PAIR_LEVEL,
        )
        right = {(0, 0): got[0], (0, 1): got[1], (1, 0): got[2], (1, 1): got[3],
                 (2, 0): got[4], (3, 0): got[5], (2, 1): got[6], (3, 1): got[7]}
        put_group(5, lt, right, low, high)
    total = column_moments(low, high)
    row = iota((8, LANES), 0)
    lane = iota((8, LANES), 1)
    meta = jnp.zeros((8, LANES), F32)
    for t in range(2):
        scalars = [mask[0, 0, t, k].astype(F32) for k in range(3)]
        scalars += [offset[0, 0, t, d, k].astype(F32) for k in range(3) for d in range(2)]
        scalars.append(stiff[0, 0, t])
        for n, value in enumerate(scalars):
            meta = jnp.where(lane == META_LANE + 2 * n + t, value, meta)
    out[...] = jnp.where((row == 2) & (lane >= META_LANE) & (lane < 64), meta, total)


def pairs_kernel(strips, lower, later, own, out, grad, misfit, low, high):
    low[...] = jnp.zeros_like(low)
    high[...] = jnp.zeros_like(high)
    for kind, image_a, second in ((0, 3, lower), (1, 4, later)):
        for t in range(2):
            a = strips[0, 0, t, image_a].astype(F32)
            b = second[t].astype(F32)
            store_gradients(a, grad.at[kind, t, 0], grad.at[kind, t, 1])
            store_gradients(b, grad.at[kind, t, 2], grad.at[kind, t, 3])
            misfit[kind, t] = a - b
        for lt in range(4):
            lanes = pl.ds(lt * LANES, LANES)
            cross, pull = {}, {}
            for t in range(2):
                g = [grad.at[kind, t, n] for n in range(4)]
                got = accumulate(pair_fields(*g, misfit.at[kind, t], lanes), PAIR_LEVEL)
                for n in range(4):
                    cross[(n, t)] = got[n]
                    pull[(n, t)] = got[4 + n]
            put_group(3 + kind, lt, cross, low, high)
            put_group(6 + kind, lt, pull, low, high)
    total = column_moments(low, high)
    row = iota((8, LANES), 0)
    lane = iota((8, LANES), 1)
    is_meta = (row == 2) & (lane >= META_LANE) & (lane < 64)
    out[...] = own[...] + jnp.where(is_meta, 0.0, total)


def solve_kernel(mine, theirs, update_out, residual_out, table):
    core = lax.axis_index("core")
    place = lax.axis_index("y") * 32 + lax.axis_index("tile")
    sub = iota((8, LANES), 0)
    lane = iota((8, LANES), 1)
    c0 = (sub & 1) == 0
    t0 = (sub & 2) == 0
    live = sub < 4
    row = lane & 31
    sec = 2 * (lane >> 5) + (sub & 1)
    for r in range(3):
        a = mine[pl.ds(r, LANES, stride=4), :]
        b = theirs[pl.ds(r, LANES, stride=4), :]
        first = jnp.where(core == 0, a, b)
        second = jnp.where(core == 0, b, a)
        table[pl.ds(256 * r, LANES, stride=2), :] = first.T
        table[pl.ds(256 * r + 1, LANES, stride=2), :] = second.T

    def read(r, h, f):
        return table[pl.ds(256 * r + 128 * h + 4 * f, 8), :]

    def low3(f):
        return read(1, 0, f), read(0, 1, f), read(0, 0, f)

    def all6(f):
        return (read(2, 0, f), read(1, 1, f), read(1, 0, f), read(2, 1, f), read(0, 1, f), read(0, 0, f))

    def meta(n):
        return read(2, 0, META_LANE // 2 + n)

    def swap_tile(x):
        return jnp.where(t0, pltpu.roll(x, 6, 0), pltpu.roll(x, 2, 0))

    def swap_core(x):
        return jnp.where(c0, pltpu.roll(x, 7, 0), pltpu.roll(x, 1, 0))

    def row_from_next(x):
        return pltpu.roll(x, LANES - 1, 1)

    def row_to_next(x):
        return pltpu.roll(x, 1, 1)

    def sec_from_next(x):
        x = swap_core(x)
        return jnp.where(c0, x, pltpu.roll(x, LANES - 32, 1))

    def sec_to_next(x):
        x = swap_core(x)
        return jnp.where(c0, pltpu.roll(x, 32, 1), x)

    zero = jnp.zeros((8, LANES), F32)
    exists_right = jnp.where((meta(0) == 1.0) & t0, 1.0, 0.0)
    exists_right = jnp.where(t0, exists_right, swap_tile(exists_right))
    exists_down = jnp.where((meta(1) == 1.0) & (row < 31), 1.0, 0.0)
    exists_sec = jnp.where((meta(2) == 1.0) & (sec < 7), 1.0, 0.0)
    du = [meta(3 + 2 * k) * (1.0 / W) for k in range(3)]
    dv = [meta(4 + 2 * k) * (1.0 / H) for k in range(3)]
    stiffness = meta(9)
    au = jnp.where(t0, zero, swap_tile(du[0]))
    av = jnp.where(t0, zero, swap_tile(dv[0]))
    bu = jnp.where(t0, du[0], zero)
    bv = jnp.where(t0, dv[0], zero)

    def shifted(m, a, b):
        uu, uv, u, vv, v, one = m
        return (uu + 2.0 * a * u + a * a * one, uv + a * v + b * u + a * b * one, u + a * one,
                vv + 2.0 * b * v + b * b * one, v + b * one, one)

    down_up, down_du, down_dv = row_to_next(exists_down), row_to_next(du[1]), row_to_next(dv[1])
    sec_up, sec_du, sec_dv = sec_to_next(exists_sec), sec_to_next(du[2]), sec_to_next(dv[2])
    blocks = []
    for n in range(3):
        total = [exists_right * m for m in shifted(all6(SELF_H + n), au, av)]
        for f, ex, off in ((SELF_T, down_up, (down_du, down_dv)), (SELF_B, exists_down, None),
                           (SELF_P, exists_sec, None), (SELF_P, sec_up, (sec_du, sec_dv))):
            m = all6(f + n)
            if off is not None:
                m = shifted(m, *off)
            total = [x + ex * y for x, y in zip(total, m)]
        if n != 1:
            total = [x + stiffness if i in (0, 3, 5) else x for i, x in enumerate(total)]
        blocks.append(total)
    square = ((0, 1, 2), (1, 3, 4), (2, 4, 5))
    diagonal = [[blocks[(i // 3) + (j // 3)][square[i % 3][j % 3]] for j in range(6)] for i in range(6)]

    lower = [[None] * 6 for _ in range(6)]
    scaled_col = [[None] * 6 for _ in range(6)]
    inverse_pivot = []
    work = {(i, j): diagonal[i][j] for i in range(6) for j in range(i + 1)}
    for j in range(6):
        inv = 1.0 / work[(j, j)]
        inverse_pivot.append(inv)
        for i in range(j + 1, 6):
            lower[i][j] = work[(i, j)] * inv
        for i in range(j + 1, 6):
            for k in range(j + 1, i + 1):
                work[(i, k)] = work[(i, k)] - lower[i][j] * work[(k, j)]
    inverse = [[None] * 6 for _ in range(6)]
    for j in range(6):
        for i in range(j + 1, 6):
            value = lower[i][j]
            for k in range(j + 1, i):
                value = value + lower[i][k] * inverse[k][j]
            inverse[i][j] = -value

    def precondition(v):
        mid = []
        for i in range(6):
            value = v[i]
            for j in range(i):
                value = value + inverse[i][j] * v[j]
            mid.append(value * inverse_pivot[i])
        out = []
        for i in range(6):
            value = mid[i]
            for j in range(i + 1, 6):
                value = value + inverse[j][i] * mid[j]
            out.append(value)
        return out

    def coupling(m, ex, ra, rb, ca, cb):
        uu, uv, u, vv, v, one = m
        if ra is None:
            block = [[uu + ca * u, uv + cb * u, u], [uv + ca * v, vv + cb * v, v], [u + ca * one, v + cb * one, one]]
        else:
            block = [[uu + (ra + ca) * u, uv + ra * v + cb * u, u + ra * one],
                     [uv + ca * v + rb * u, vv + (rb + cb) * v, v + rb * one],
                     [u + ca * one, v + cb * one, one]]
        return [[-(ex * x) for x in line] for line in block]

    def join(xx, xy, yx, yy):
        return [a + b for a, b in zip(xx, xy)] + [a + b for a, b in zip(yx, yy)]

    couplings = {}
    for kind, n, ex in (("down", 1, exists_down), ("sec", 2, exists_sec)):
        f = CROSS[kind]
        couplings[kind] = join(*(coupling(all6(f + i), ex, None, None, du[n], dv[n]) for i in range(4)))
    a6, b6 = all6(CROSS_RIGHT), all6(CROSS_RIGHT + 1)
    sa6, sb6 = [swap_tile(x) for x in a6], [swap_tile(x) for x in b6]

    def pick(x, y):
        return [jnp.where(t0, p, q) for p, q in zip(x, y)]

    right = (pick(a6, sa6), pick(sa6, sb6), pick(b6, a6), pick(sb6, b6))
    right = join(*(coupling(m, exists_right, au, av, bu, bv) for m in right))

    sign = jnp.where(t0, -2.0, 2.0) * exists_right
    load = []
    for n in range(2):
        u, v, one = low3(PULL_RIGHT + n)
        load += [sign * (u + au * one), sign * (v + av * one), sign * one]
    for kind, n, ex, push in (("down", 1, exists_down, row_to_next), ("sec", 2, exists_sec, sec_to_next)):
        f = PULL[kind]
        twice = 2.0 * ex
        for i in range(2):
            for j, x in enumerate(low3(f + i)):
                load[3 * i + j] = load[3 * i + j] - twice * x
            u, v, one = low3(f + 2 + i)
            for j, x in enumerate((u + du[n] * one, v + dv[n] * one, one)):
                load[3 * i + j] = load[3 * i + j] + push(twice * x)

    def times(block, vector, transpose):
        out = []
        for i in range(6):
            value = None
            for j in range(6):
                term = (block[j][i] if transpose else block[i][j]) * vector[j]
                value = term if value is None else value + term
            out.append(value)
        return out

    def multiply(vector):
        parts = [times(diagonal, vector, False)]
        parts.append(times(right, [swap_tile(x) for x in vector], False))
        parts.append(times(couplings["down"], [row_from_next(x) for x in vector], False))
        parts.append([row_to_next(x) for x in times(couplings["down"], vector, True)])
        parts.append(times(couplings["sec"], [sec_from_next(x) for x in vector], False))
        parts.append([sec_to_next(x) for x in times(couplings["sec"], vector, True)])
        return [functools.reduce(jnp.add, line) for line in zip(*parts)]

    def inner(x, y):
        total = functools.reduce(jnp.add, [a * b for a, b in zip(x, y)])
        total = jnp.where(live, total, 0.0)
        return jnp.sum(total, axis=(0, 1), keepdims=True)

    residual = load
    direction = precondition(residual)
    rho = inner(residual, direction)
    update = None
    for step in range(ITERS):
        product = multiply(direction)
        size = rho / inner(direction, product)
        if update is None:
            update = [size * d for d in direction]
        else:
            update = [x + size * d for x, d in zip(update, direction)]
        residual = [r - size * p for r, p in zip(residual, product)]
        if step < ITERS - 1:
            scaled = precondition(residual)
            rho_next = inner(residual, scaled)
            ratio = rho_next / rho
            direction = [z + ratio * d for z, d in zip(scaled, direction)]
            rho = rho_next

    here = (lane == place) & live & ((sub & 1) == core)
    for vector, out in ((update, update_out), (residual, residual_out)):
        found = zero
        for i in range(6):
            value = jnp.sum(jnp.where(here, vector[i], 0.0), axis=1, keepdims=True)
            found = jnp.where(lane == i, value, found)
        found = found + pltpu.roll(found, 7, 0)
        out[0, 0, 0:1] = found[0:1, :6]
        out[0, 0, 1:2] = found[2:3, :6]


def shards(tile_strips, pair_mask, strip_offset, stiffness):
    tiles = lax.axis_size("tile")
    chips = lax.axis_size("y") * tiles
    sections = lax.axis_size("y") * 2
    image = jax.ShapeDtypeStruct((2, H, W), tile_strips.dtype)
    tops, patches = pl.pallas_call(
        cut_kernel,
        out_shape=(image, image),
        in_specs=[pl.BlockSpec(memory_space=pltpu.HBM)],
        out_specs=(VMEM, VMEM),
        scratch_shapes=[pltpu.SemaphoreType.DMA((4,))],
        compiler_params=pltpu.CompilerParams(vmem_limit_bytes=2 << 20),
        name="cut",
    )(tile_strips)
    lower = lax.ppermute(tops, "tile", [(i + 1, i) for i in range(tiles - 1)])
    later = lax.ppermute(patches, ("y", "core"), [(i + 1, i) for i in range(sections - 1)])
    small = jax.ShapeDtypeStruct((8, LANES), F32)
    own = pl.pallas_call(
        own_kernel,
        out_shape=small,
        in_specs=[VMEM, SMEM, SMEM, SMEM],
        out_specs=VMEM,
        scratch_shapes=[pltpu.VMEM((4, 2, 2, H, W), F32), pltpu.VMEM((H, W), F32),
                        pltpu.VMEM((128, W), F32), pltpu.VMEM((128, W), F32)],
        cost_estimate=pl.CostEstimate(flops=20_000_000, bytes_accessed=700_000, transcendentals=0),
        compiler_params=pltpu.CompilerParams(vmem_limit_bytes=6 << 20),
        name="own_moments",
    )(tile_strips, pair_mask, jnp.swapaxes(strip_offset, 3, 4), stiffness)
    moments = pl.pallas_call(
        pairs_kernel,
        out_shape=small,
        in_specs=[VMEM] * 4,
        out_specs=VMEM,
        scratch_shapes=[pltpu.VMEM((2, 2, 4, H, W), F32), pltpu.VMEM((2, 2, H, W), F32),
                        pltpu.VMEM((128, W), F32), pltpu.VMEM((128, W), F32)],
        cost_estimate=pl.CostEstimate(flops=20_000_000, bytes_accessed=900_000, transcendentals=0),
        compiler_params=pltpu.CompilerParams(vmem_limit_bytes=6 << 20),
        name="pair_moments",
    )(tile_strips, lower, later, own)
    sent = jnp.broadcast_to(moments[None, :4], (chips, 4, LANES))
    mine = lax.all_to_all(sent, ("y", "tile"), 0, 0)
    theirs = lax.ppermute(mine, "core", [(0, 1), (1, 0)])
    out = jax.ShapeDtypeStruct((1, 1, 2, 6), F32)
    outs = pl.pallas_call(
        solve_kernel,
        out_shape=(out, out),
        in_specs=[VMEM] * 2,
        out_specs=(VMEM, VMEM),
        scratch_shapes=[pltpu.VMEM((3 * 256 + 8, LANES), F32)],
        compiler_params=pltpu.CompilerParams(vmem_limit_bytes=4 << 20),
        name="solve",
    )(mine.reshape(chips * 4, LANES), theirs.reshape(chips * 4, LANES))
    return tuple(jnp.transpose(x, (3, 0, 1, 2)) for x in outs)


def solution(mesh):
    fine = Mesh(mesh.devices.reshape(4, 2, 32), ("y", "core", "tile"))
    sec = ("y", "core")
    return jax.shard_map(
        shards,
        mesh=fine,
        in_specs=(
            P(sec, "tile", None, None, None, None),
            P(sec, "tile", None, None),
            P(sec, "tile", None, None, None),
            P(sec, "tile", None),
        ),
        out_specs=(P(None, sec, "tile", None), P(None, sec, "tile", None)),
        check_vma=False,
    )
```

```python
import functools

import jax
import jax.numpy as jnp
from jax import lax
from jax.experimental import pallas as pl
from jax.experimental.pallas import tpu as pltpu
from jax.sharding import Mesh, PartitionSpec as P

ITERS = 3
H, W = 64, 512
F32 = jnp.float32
LANES = 128
RIGHT, CROSS, PULL, AGAIN = 24, (32, 40), (48, 56), 64
MOMENTS = 3 * W
ROWS = 2 * H + 8
SCALE = 2.0**-17

PACK_LIMIT = 2 << 20

VMEM = pl.BlockSpec(memory_space=pltpu.VMEM)
SMEM = pl.BlockSpec(memory_space=pltpu.SMEM)


def iota(shape, axis):
    return lax.broadcasted_iota(jnp.int32, shape, axis)


def store_gradients(image, gx_ref, gy_ref):
    col = iota((H, W), 1)
    row = iota((H, W), 0)
    ahead = jnp.where(col < W - 1, pltpu.roll(image, W - 1, 1), 0.0)
    behind = jnp.where(col > 0, pltpu.roll(image, 1, 1), 0.0)
    gx_ref[...] = ahead - behind
    below = jnp.where(row < H - 1, pltpu.roll(image, H - 1, 0), 0.0)
    above = jnp.where(row > 0, pltpu.roll(image, 1, 0), 0.0)
    gy_ref[...] = below - above


def row_moments(sums, level):
    s = iota((8, LANES), 0).astype(F32)
    c = 0.5 + s / H
    out = [sums[0], c * sums[0] - sums[1] * 0.125]
    if level == 3:
        out.append(c * c * sums[0] - (0.25 * c) * sums[1] + (2.0 * sums[2] - sums[1]) * (1.0 / 64.0))
    return out


def accumulate(fields, level):
    sums = None
    for k in range(8):
        values = fields(k)
        if sums is None:
            sums = [[v] * lv for v, lv in zip(values, level)]
            continue
        new = []
        for v, old, lv in zip(values, sums, level):
            now = [old[0] + v]
            for q in range(1, lv):
                now.append(old[q] + now[q - 1])
            new.append(now)
        sums = new
    return [row_moments(s, lv) for s, lv in zip(sums, level)]


def tree8(vs):
    s = iota((8, LANES), 0)
    m4 = s < 4
    w = []
    for i in range(4):
        x = jnp.where(m4, vs[i], vs[i + 4])
        y = jnp.where(m4, vs[i + 4], vs[i])
        w.append(x + pltpu.roll(y, 4, 0))
    m2 = (s & 2) == 0
    z = []
    for i in range(2):
        x = jnp.where(m2, w[i], w[i + 2])
        y = jnp.where(m2, w[i + 2], w[i])
        z.append(x + jnp.where(m2, pltpu.roll(y, 6, 0), pltpu.roll(y, 2, 0)))
    m1 = (s & 1) == 0
    x = jnp.where(m1, z[0], z[1])
    y = jnp.where(m1, z[1], z[0])
    return x + jnp.where(m1, pltpu.roll(y, 7, 0), pltpu.roll(y, 1, 0))


def put_group(group, lt, found, table):
    order = [found[(f, t)] for f in range(4) for t in range(2)]
    for q in range(3):
        vs = [v[q] if len(v) > q else None for v in order]
        rows = pl.ds(8 * group, 8), pl.ds(q * W + lt * LANES, LANES)
        if all(v is None for v in vs):
            table[rows] = jnp.zeros((8, LANES), F32)
        else:
            table[rows] = tree8([jnp.zeros((8, LANES), F32) if v is None else v for v in vs])


def column_moments(table, wide):
    r = iota((8, MOMENTS), 0)
    j = iota((8, MOMENTS), 1)
    u = (j & (W - 1)).astype(F32) / W - 0.5
    q = j // W
    one = ((r == 0) & (q == 0)) | ((r == 2) & (q == 1)) | ((r == 5) & (q == 2))
    first = ((r == 1) & (q == 0)) | ((r == 4) & (q == 1))
    weight = jnp.where(one, 1.0, jnp.where(first, u, jnp.where((r == 3) & (q == 0), u * u, 0.0))) * SCALE
    dims = (((1,), (1,)), ((), ()))
    wide[...] = jnp.zeros_like(wide)
    wide[:, 0 : table.shape[0]] = lax.dot_general(
        weight, table[...], dims, precision=lax.Precision.HIGHEST, preferred_element_type=F32
    )
    return wide[...]


def pair_fields(gxa, gya, gxb, gyb, misfit, lanes):
    def fields(k):
        rows = pl.ds(8 * k, 8)
        xa, ya, xb, yb, m = (ref[rows, lanes] for ref in (gxa, gya, gxb, gyb, misfit))
        return [xa * xb, xa * yb, ya * xb, ya * yb, xa * m, ya * m, xb * m, yb * m]

    return fields


def self_fields(gx, gy, lanes):
    def fields(k):
        rows = pl.ds(8 * k, 8)
        x, y = gx[rows, lanes], gy[rows, lanes]
        return [x * x, x * y, y * y]

    return fields


PAIR_LEVEL = (3, 3, 3, 3, 2, 2, 2, 2)


def by_tile(values, shape=(8, LANES)):
    return jnp.where((iota(shape, 1) & 1) == 0, values[0], values[1])


def in_range(lane, start, length):
    return (lane >= start) & (lane < start + length)


def own_exists(mask):
    down = lax.axis_index("tile") < 31
    sec = 2 * lax.axis_index("y") + lax.axis_index("core") < 7
    out = []
    for k, inside in ((1, down), (2, sec)):
        out.append([jnp.where((mask[0, 0, t, k] == 1) & inside, 1.0, 0.0) for t in range(2)])
    return out


def pack_kernel(strips, mask_in, offset_in, bottoms, patches, mask, offset, sems, small_sems):
    small = [pltpu.make_async_copy(mask_in, mask, small_sems.at[0]),
             pltpu.make_async_copy(offset_in, offset, small_sems.at[1])]
    for copy in small:
        copy.start()
    copies = []
    for n, (ref, image) in enumerate(((bottoms, 3), (patches, 4))):
        for t in range(2):
            copies.append(
                pltpu.make_async_copy(strips.at[0, 0, t, image], ref.at[pl.ds(H * t, H)], sems.at[2 * n + t])
            )
    for copy in copies:
        copy.start()
    for copy in small:
        copy.wait()
    exists = own_exists(mask)
    row = iota((8, W), 0)
    for n, ref in enumerate((bottoms, patches)):
        lines = [by_tile(exists[n], (8, W))]
        for d in range(2):
            lines.append(by_tile([offset[0, 0, t, d, n + 1].astype(F32) for t in range(2)], (8, W)))
        block = jnp.where(row == 0, lines[0], jnp.where(row == 1, lines[1], jnp.where(row == 2, lines[2], 0.0)))
        ref[2 * H :, :] = block.astype(jnp.bfloat16)
    for copy in copies:
        copy.wait()


def own_kernel(strips, mask, offset, stiff, out, facts, second, grad, misfit, table, wide):
    kinds = ((1, 0), (3, 3), (4, 4), (2, 2))
    refs = {}
    for kind, images in enumerate(kinds):
        for t in range(2):
            home = grad.at[kind, t] if kind < 2 else second.at[3 - kind, t]
            refs[(kind, t)] = (home.at[0], home.at[1])
            store_gradients(strips[0, 0, t, images[t]].astype(F32), *refs[(kind, t)])
    misfit[...] = strips[0, 0, 0, 1].astype(F32) - strips[0, 0, 1, 0].astype(F32)
    for lt in range(4):
        lanes = pl.ds(lt * LANES, LANES)
        found = {}
        for kind in range(4):
            for t in range(2):
                got = accumulate(self_fields(*refs[(kind, t)], lanes), (3, 3, 3))
                for n in range(3):
                    found[(3 * kind + n, t)] = got[n]
        for group in range(3):
            put_group(group, lt, {(f, t): found[(4 * group + f, t)] for f in range(4) for t in range(2)}, table)
        got = accumulate(pair_fields(*refs[(0, 0)], *refs[(0, 1)], misfit, lanes), PAIR_LEVEL)
        right = {(0, 0): got[0], (0, 1): got[1], (1, 0): got[2], (1, 1): got[3],
                 (2, 0): got[4], (3, 0): got[5], (2, 1): got[6], (3, 1): got[7]}
        put_group(3, lt, right, table)
    out[...] = column_moments(table, wide)
    row = iota((8, LANES), 0)
    lane = iota((8, LANES), 1)
    even = (lane & 1) == 0
    down, sec = own_exists(mask)
    right = jnp.where(mask[0, 0, 0, 0] == 1, 1.0, 0.0)
    pull = in_range(lane, RIGHT + 4, 4)
    factor = jnp.where(lane < 6, right, 0.0)
    factor = jnp.where(in_range(lane, 6, 6), by_tile(down), factor)
    factor = jnp.where(in_range(lane, 12, 6), by_tile(sec), factor)
    factor = jnp.where(in_range(lane, RIGHT, 4), -right, factor)
    factor = jnp.where(pull, jnp.where(even, -2.0, 2.0) * right, factor)
    shift = [offset[0, 0, 0, d, 0].astype(F32) for d in range(2)]
    moved = (~even) & ((lane < 6) | pull)
    lines = [factor]
    lines += [jnp.where(moved, shift[d], 0.0) for d in range(2)]
    lines += [by_tile([stiff[0, 0, t] for t in range(2)])]
    lines += [jnp.full((8, LANES), shift[d], F32) for d in range(2)]
    total = jnp.zeros((8, LANES), F32)
    for n, line in enumerate(lines):
        total = jnp.where(row == n, line, total)
    facts[...] = total


def pair_moments(kind, strips, sent, second, grad, misfit, table, wide):
    for t in range(2):
        a = sent[H * t : H * (t + 1), :].astype(F32)
        store_gradients(a, grad.at[t, 0], grad.at[t, 1])
        misfit[t] = a - strips[0, 0, t, (2, 4)[kind]].astype(F32)
    for lt in range(4):
        lanes = pl.ds(lt * LANES, LANES)
        cross, pull = {}, {}
        for t in range(2):
            g = [grad.at[t, 0], grad.at[t, 1], second.at[kind, t, 0], second.at[kind, t, 1]]
            got = accumulate(pair_fields(*g, misfit.at[t], lanes), PAIR_LEVEL)
            for n in range(4):
                cross[(n, t)] = got[n]
                pull[(n, t)] = got[4 + n]
        put_group(0, lt, cross, table)
        put_group(1, lt, pull, table)
    found = column_moments(table, wide)
    lane = iota((8, LANES), 1)
    moved = jnp.where(in_range(lane, PULL[kind], 8), pltpu.roll(found, PULL[kind] - 8, 1), 0.0)
    return jnp.where(in_range(lane, CROSS[kind], 8), pltpu.roll(found, CROSS[kind], 1), moved)


def down_kernel(strips, upper, second, own, out, grad, misfit, table, wide):
    out[...] = own[...] + pair_moments(0, strips, upper, second, grad, misfit, table, wide)


def sec_kernel(strips, upper, before, second, own, facts, out, grad, misfit, table, wide):
    moments = own[...] + pair_moments(1, strips, before, second, grad, misfit, table, wide)
    lane = iota((1, LANES), 1)
    wide_lane = iota((8, LANES), 1)
    moments = moments + jnp.where(in_range(wide_lane, AGAIN, 6), pltpu.roll(moments, AGAIN - 12, 1), 0.0)
    factor, au, av = facts[0:1, :], facts[1:2, :], facts[2:3, :]
    told = []
    for kind, sent in enumerate((upper, before)):
        known = sent[2 * H :, 0:LANES].astype(F32)
        exists, dx, dy = known[0:1], known[1:2], known[2:3]
        told += [dx, dy]
        alone = in_range(lane, (18, AGAIN)[kind], 6)
        pull_b = in_range(lane, PULL[kind] + 4, 4)
        factor = jnp.where(alone, exists, factor)
        factor = jnp.where(in_range(lane, CROSS[kind], 8), -exists, factor)
        factor = jnp.where(in_range(lane, PULL[kind], 4), -2.0 * exists, factor)
        factor = jnp.where(pull_b, 2.0 * exists, factor)
        au = jnp.where(alone | pull_b, dx, au)
        av = jnp.where(alone | pull_b, dy, av)
    au = au * (1.0 / W)
    av = av * (1.0 / H)
    one, u, v, uu, uv, vv = (moments[n : n + 1, :] for n in range(6))
    lines = [one, u + au * one, v + av * one, uu + 2.0 * au * u + au * au * one,
             uv + au * v + av * u + au * av * one, vv + 2.0 * av * v + av * av * one]
    row = iota((8, LANES), 0)
    full = jnp.zeros((8, LANES), F32)
    for n, line in enumerate(lines):
        full = jnp.where(row == n, line * factor, full)

    def back(x, by):
        return pltpu.roll(x, LANES - by, 1)

    alone = full + back(full, 6) + back(full, 12) + back(full, 18) + back(full, AGAIN)
    alone = pltpu.roll(alone, 58, 1)
    ends = in_range(wide_lane, 58, 2) | in_range(wide_lane, 62, 2)
    alone = jnp.where(ends & ((row == 0) | (row == 3) | (row == 5)), alone + facts[3:4, :], alone)
    load = full + back(full, 24) + back(full, 32)
    final = jnp.where(in_range(wide_lane, 28, 4), load, full)
    final = jnp.where(in_range(wide_lane, 52, 4), back(full, 4), final)
    final = jnp.where(in_range(wide_lane, 58, 6), alone, final)
    tail = (told, [facts[4:5, :], facts[5:6, :]])
    for r in range(2):
        line = jnp.zeros((1, LANES), F32)
        for n, value in enumerate(tail[r]):
            line = jnp.where(in_range(lane, 120 + 2 * n, 2), value, line)
        for n, move in ((2, 56), (1, 16), (0, 104)):
            part = pltpu.roll(final, move, 1)[3 * r + n : 3 * r + n + 1, :]
            line = jnp.where(in_range(lane, 40 * n, 40), part, line)
        out[r : r + 1, :] = line


def solve_kernel(mine, theirs, update_out, residual_out, table):
    core = lax.axis_index("core")
    place = lax.axis_index("y") * 32 + lax.axis_index("tile")
    sub = iota((8, LANES), 0)
    lane = iota((8, LANES), 1)
    c0 = (sub & 1) == 0
    t0 = (sub & 2) == 0
    live = sub < 4
    for r in range(2):
        a = mine[pl.ds(r, LANES, stride=2), :]
        b = theirs[pl.ds(r, LANES, stride=2), :]
        first = jnp.where(core == 0, a, b)
        second = jnp.where(core == 0, b, a)
        table[pl.ds(256 * r, LANES, stride=2), :] = first.T
        table[pl.ds(256 * r + 1, LANES, stride=2), :] = second.T

    def read(r, place):
        return table[pl.ds(256 * r + 4 * place, 8), :]

    def low3(place):
        return read(0, 20 + place), read(0, 40 + place), read(0, place)

    def all6(place):
        return (read(1, place), read(1, 20 + place), read(0, 20 + place), read(1, 40 + place),
                read(0, 40 + place), read(0, place))

    def swap_tile(x):
        return jnp.where(t0, pltpu.roll(x, 6, 0), pltpu.roll(x, 2, 0))

    def swap_core(x):
        return jnp.where(c0, pltpu.roll(x, 7, 0), pltpu.roll(x, 1, 0))

    def row_from_next(x):
        return pltpu.roll(x, LANES - 1, 1)

    def row_to_next(x):
        return pltpu.roll(x, 1, 1)

    def sec_from_next(x):
        x = swap_core(x)
        return jnp.where(c0, x, pltpu.roll(x, LANES - 32, 1))

    def sec_to_next(x):
        x = swap_core(x)
        return jnp.where(c0, pltpu.roll(x, 32, 1), x)

    zero = jnp.zeros((8, LANES), F32)
    du = [read(1, 60) * (1.0 / W), read(0, 60) * (1.0 / W), read(0, 62) * (1.0 / W)]
    dv = [read(1, 61) * (1.0 / H), read(0, 61) * (1.0 / H), read(0, 63) * (1.0 / H)]
    au = jnp.where(t0, zero, du[0])
    av = jnp.where(t0, zero, dv[0])
    bu = jnp.where(t0, du[0], zero)
    bv = jnp.where(t0, dv[0], zero)
    blocks = [all6(17 + n) for n in range(3)]
    square = ((0, 1, 2), (1, 3, 4), (2, 4, 5))
    diagonal = [[blocks[(i // 3) + (j // 3)][square[i % 3][j % 3]] for j in range(6)] for i in range(6)]

    lower = [[None] * 6 for _ in range(6)]
    scaled_col = [[None] * 6 for _ in range(6)]
    inverse_pivot = []
    work = {(i, j): diagonal[i][j] for i in range(6) for j in range(i + 1)}
    for j in range(6):
        inv = 1.0 / work[(j, j)]
        inverse_pivot.append(inv)
        for i in range(j + 1, 6):
            lower[i][j] = work[(i, j)] * inv
        for i in range(j + 1, 6):
            for k in range(j + 1, i + 1):
                work[(i, k)] = work[(i, k)] - lower[i][j] * work[(k, j)]
    inverse = [[None] * 6 for _ in range(6)]
    for j in range(6):
        for i in range(j + 1, 6):
            value = lower[i][j]
            for k in range(j + 1, i):
                value = value + lower[i][k] * inverse[k][j]
            inverse[i][j] = -value

    def precondition(v):
        mid = []
        for i in range(6):
            value = v[i]
            for j in range(i):
                value = value + inverse[i][j] * v[j]
            mid.append(value * inverse_pivot[i])
        out = []
        for i in range(6):
            value = mid[i]
            for j in range(i + 1, 6):
                value = value + inverse[j][i] * mid[j]
            out.append(value)
        return out

    def coupling(m, ra, rb, ca, cb):
        uu, uv, u, vv, v, one = m
        if ra is None:
            return [[uu + ca * u, uv + cb * u, u], [uv + ca * v, vv + cb * v, v], [u + ca * one, v + cb * one, one]]
        return [[uu + (ra + ca) * u, uv + ra * v + cb * u, u + ra * one],
                [uv + ca * v + rb * u, vv + (rb + cb) * v, v + rb * one],
                [u + ca * one, v + cb * one, one]]

    def join(xx, xy, yx, yy):
        return [a + b for a, b in zip(xx, xy)] + [a + b for a, b in zip(yx, yy)]

    down, across = (
        join(*(coupling(all6(place + i), None, None, du[n], dv[n]) for i in range(4))) for n, place in ((1, 4), (2, 8))
    )
    a6, b6 = all6(0), all6(1)
    sa6, sb6 = [swap_tile(x) for x in a6], [swap_tile(x) for x in b6]

    def pick(x, y):
        return [jnp.where(t0, p, q) for p, q in zip(x, y)]

    right = (pick(a6, sa6), pick(sa6, sb6), pick(b6, a6), pick(sb6, b6))
    right = join(*(coupling(m, au, av, bu, bv) for m in right))

    load = []
    for n in range(2):
        for x, y, z in zip(low3(2 + n), low3(12 + n), low3(14 + n)):
            load.append(x + row_from_next(y) + sec_from_next(z))

    def times(block, vector, transpose):
        out = []
        for i in range(6):
            value = None
            for j in range(6):
                term = (block[j][i] if transpose else block[i][j]) * vector[j]
                value = term if value is None else value + term
            out.append(value)
        return out

    def multiply(vector):
        parts = [times(diagonal, vector, False)]
        parts.append(times(right, [swap_tile(x) for x in vector], False))
        parts.append([row_from_next(x) for x in times(down, vector, False)])
        parts.append(times(down, [row_to_next(x) for x in vector], True))
        parts.append([sec_from_next(x) for x in times(across, vector, False)])
        parts.append(times(across, [sec_to_next(x) for x in vector], True))
        return [functools.reduce(jnp.add, line) for line in zip(*parts)]

    def inner(x, y):
        total = functools.reduce(jnp.add, [a * b for a, b in zip(x, y)])
        total = jnp.where(live, total, 0.0)
        return jnp.sum(total, axis=(0, 1), keepdims=True)

    residual = load
    direction = precondition(residual)
    rho = inner(residual, direction)
    update = None
    for step in range(ITERS):
        product = multiply(direction)
        size = rho / inner(direction, product)
        if update is None:
            update = [size * d for d in direction]
        else:
            update = [x + size * d for x, d in zip(update, direction)]
        residual = [r - size * p for r, p in zip(residual, product)]
        if step < ITERS - 1:
            scaled = precondition(residual)
            rho_next = inner(residual, scaled)
            ratio = rho_next / rho
            direction = [z + ratio * d for z, d in zip(scaled, direction)]
            rho = rho_next

    here = (lane == place) & live & ((sub & 1) == core)
    for vector, out in ((update, update_out), (residual, residual_out)):
        found = zero
        for i in range(6):
            value = jnp.sum(jnp.where(here, vector[i], 0.0), axis=1, keepdims=True)
            found = jnp.where(lane == i, value, found)
        found = found + pltpu.roll(found, 7, 0)
        out[0, 0, 0:1] = found[0:1, :6]
        out[0, 0, 1:2] = found[2:3, :6]


def shards(tile_strips, pair_mask, strip_offset, stiffness):
    tiles = lax.axis_size("tile")
    chips = lax.axis_size("y") * tiles
    sections = lax.axis_size("y") * 2
    offset = jnp.swapaxes(strip_offset, 3, 4)
    image = jax.ShapeDtypeStruct((ROWS, W), tile_strips.dtype)
    bottoms, patches = pl.pallas_call(
        pack_kernel,
        out_shape=(image, image),
        in_specs=[pl.BlockSpec(memory_space=pltpu.HBM)] * 3,
        out_specs=(VMEM, VMEM),
        scratch_shapes=[pltpu.SMEM(pair_mask.shape, jnp.int32), pltpu.SMEM(offset.shape, jnp.int32),
                        pltpu.SemaphoreType.DMA((4,)), pltpu.SemaphoreType.DMA((2,))],
        cost_estimate=pl.CostEstimate(flops=0, bytes_accessed=0, transcendentals=0),
        compiler_params=pltpu.CompilerParams(vmem_limit_bytes=PACK_LIMIT),
        name="pack",
    )(*(pltpu.with_memory_space_constraint(x, pltpu.HBM) for x in (tile_strips, pair_mask, offset)))
    upper = lax.ppermute(bottoms, "tile", [(i, i + 1) for i in range(tiles - 1)])
    before = lax.ppermute(patches, ("y", "core"), [(i, i + 1) for i in range(sections - 1)])
    small = jax.ShapeDtypeStruct((8, LANES), F32)
    wide = pltpu.VMEM((8, LANES), F32)
    params = pltpu.CompilerParams(vmem_limit_bytes=6 << 20)
    own, facts, second = pl.pallas_call(
        own_kernel,
        out_shape=(small, small, jax.ShapeDtypeStruct((2, 2, 2, H, W), F32)),
        in_specs=[VMEM, SMEM, SMEM, SMEM],
        out_specs=(VMEM, VMEM, VMEM),
        scratch_shapes=[pltpu.VMEM((2, 2, 2, H, W), F32), pltpu.VMEM((H, W), F32), pltpu.VMEM((32, MOMENTS), F32), wide],
        cost_estimate=pl.CostEstimate(flops=20_000_000, bytes_accessed=700_000, transcendentals=0),
        compiler_params=params,
        name="own_moments",
    )(tile_strips, pair_mask, offset, stiffness)
    scratch = [pltpu.VMEM((2, 2, H, W), F32), pltpu.VMEM((2, H, W), F32), pltpu.VMEM((16, MOMENTS), F32), wide]
    cost = pl.CostEstimate(flops=10_000_000, bytes_accessed=900_000, transcendentals=0)
    own = pl.pallas_call(
        down_kernel,
        out_shape=small,
        in_specs=[VMEM] * 4,
        out_specs=VMEM,
        scratch_shapes=scratch,
        cost_estimate=cost,
        compiler_params=params,
        name="down_moments",
    )(tile_strips, upper, second, own)
    message = pl.pallas_call(
        sec_kernel,
        out_shape=jax.ShapeDtypeStruct((2, LANES), F32),
        in_specs=[VMEM] * 6,
        out_specs=VMEM,
        scratch_shapes=scratch,
        cost_estimate=cost,
        compiler_params=params,
        name="sec_moments",
    )(tile_strips, upper, before, second, own, facts)
    sent = jnp.broadcast_to(message[None], (chips, 2, LANES))
    mine = lax.all_to_all(sent, ("y", "tile"), 0, 0)
    theirs = lax.ppermute(mine, "core", [(0, 1), (1, 0)])
    out = jax.ShapeDtypeStruct((1, 1, 2, 6), F32)
    outs = pl.pallas_call(
        solve_kernel,
        out_shape=(out, out),
        in_specs=[VMEM] * 2,
        out_specs=(VMEM, VMEM),
        scratch_shapes=[pltpu.VMEM((2 * 256 + 8, LANES), F32)],
        compiler_params=pltpu.CompilerParams(vmem_limit_bytes=4 << 20),
        name="solve",
    )(mine.reshape(chips * 2, LANES), theirs.reshape(chips * 2, LANES))
    return tuple(jnp.transpose(x, (3, 0, 1, 2)) for x in outs)


def solution(mesh):
    fine = Mesh(mesh.devices.reshape(4, 2, 32), ("y", "core", "tile"))
    sec = ("y", "core")
    return jax.shard_map(
        shards,
        mesh=fine,
        in_specs=(
            P(sec, "tile", None, None, None, None),
            P(sec, "tile", None, None),
            P(sec, "tile", None, None, None),
            P(sec, "tile", None),
        ),
        out_specs=(P(None, sec, "tile", None), P(None, sec, "tile", None)),
        check_vma=False,
    )
```

```python
import functools

import jax
import jax.numpy as jnp
from jax import lax
from jax.experimental import pallas as pl
from jax.experimental.pallas import tpu as pltpu
from jax.sharding import Mesh, PartitionSpec as P

ITERS = 3
H, W = 64, 512
F32 = jnp.float32
LANES = 128
RIGHT, CROSS, PULL, AGAIN = 24, (32, 40), (48, 56), 64
ROWS = 2 * H + 8
SCALE = 2.0**-17

PACK_LIMIT = 2 << 20

VMEM = pl.BlockSpec(memory_space=pltpu.VMEM)
SMEM = pl.BlockSpec(memory_space=pltpu.SMEM)


def iota(shape, axis):
    return lax.broadcasted_iota(jnp.int32, shape, axis)


def store_gradients(image, gx_ref, gy_ref, pad):
    lane = iota((8, LANES), 1)
    inner_first, inner_last = lane > 0, lane < LANES - 1
    zero = jnp.zeros((8, LANES), F32)
    tiles = []
    for lt in range(4):
        x = image(lt)
        pad[lt, 0:8] = zero
        pad[lt, 8 : 8 + H] = x
        pad[lt, 8 + H : 16 + H] = zero
        tiles.append([x[8 * k : 8 * k + 8] for k in range(8)])
    for k in range(8):
        ahead = [pltpu.roll(tiles[lt][k], LANES - 1, 1) for lt in range(4)] + [zero]
        behind = [zero] + [pltpu.roll(tiles[lt][k], 1, 1) for lt in range(4)]
        for lt in range(4):
            here = pl.ds(8 * k, 8), pl.ds(lt * LANES, LANES)
            gx_ref[here] = jnp.where(inner_last, ahead[lt], ahead[lt + 1]) - jnp.where(
                inner_first, behind[lt + 1], behind[lt]
            )
            gy_ref[here] = pad[lt, 9 + 8 * k : 17 + 8 * k] - pad[lt, 7 + 8 * k : 15 + 8 * k]


def row_moments(sums, level):
    c = 0.5 + iota((8, LANES), 0).astype(F32) / H
    out = [sums[0], c * sums[0] - sums[1] * 0.125]
    if level == 3:
        out.append((c * c) * sums[0] - (0.25 * c + 1.0 / 64.0) * sums[1] + sums[2] * (1.0 / 32.0))
    return out


def accumulate(fields, level):
    sums = None
    for k in range(8):
        values = fields(k)
        if sums is None:
            sums = [[v] * lv for v, lv in zip(values, level)]
            continue
        new = []
        for v, old, lv in zip(values, sums, level):
            now = [old[0] + v]
            for q in range(1, lv):
                now.append(old[q] + now[q - 1])
            new.append(now)
        sums = new
    return [row_moments(s, lv) for s, lv in zip(sums, level)]


def tree8(vs):
    s = iota((8, LANES), 0)
    m4 = s < 4
    w = []
    for i in range(4):
        x = jnp.where(m4, vs[i], vs[i + 4])
        y = jnp.where(m4, vs[i + 4], vs[i])
        w.append(x + pltpu.roll(y, 4, 0))
    m2 = (s & 2) == 0
    z = []
    for i in range(2):
        x = jnp.where(m2, w[i], w[i + 2])
        y = jnp.where(m2, w[i + 2], w[i])
        z.append(x + jnp.where(m2, pltpu.roll(y, 6, 0), pltpu.roll(y, 2, 0)))
    m1 = (s & 1) == 0
    x = jnp.where(m1, z[0], z[1])
    y = jnp.where(m1, z[1], z[0])
    return x + jnp.where(m1, pltpu.roll(y, 7, 0), pltpu.roll(y, 1, 0))


def put_group(group, lt, found, total):
    order = [found[(f, t)] for f in range(4) for t in range(2)]
    low = [tree8([v[q] for v in order]) for q in range(2)]
    u = (iota((8, LANES), 1) + lt * LANES).astype(F32) / W - 0.5
    new = [low[0], u * low[0], low[1]]
    if any(len(v) > 2 for v in order):
        zero = jnp.zeros((8, LANES), F32)
        new += [(u * u) * low[0], u * low[1], tree8([v[2] if len(v) > 2 else zero for v in order])]
    for m, value in enumerate(new):
        total[(m, group)] = total[(m, group)] + value if lt else value


def column_moments(total, groups, table, wide):
    dims = (((1,), (1,)), ((), ()))
    zero = jnp.zeros((8, LANES), F32)
    scale = jnp.full((8, LANES), SCALE, F32)
    row = iota((8, 8 * groups), 0)
    out = None
    for m in range(6):
        for group in range(groups):
            table[m, pl.ds(8 * group, 8)] = total.get((m, group), zero)
        part = lax.dot_general(
            scale, table[m], dims, precision=lax.Precision.HIGHEST, preferred_element_type=F32
        )
        out = part if out is None else jnp.where(row == m, part, out)
    wide[...] = zero
    wide[0:6, 0 : 8 * groups] = out[0:6]
    return wide[...]


def pair_fields(gxa, gya, gxb, gyb, misfit, lanes):
    def fields(k):
        rows = pl.ds(8 * k, 8)
        xa, ya, xb, yb, m = (ref[rows, lanes] for ref in (gxa, gya, gxb, gyb, misfit))
        return [xa * xb, xa * yb, ya * xb, ya * yb, xa * m, ya * m, xb * m, yb * m]

    return fields


def self_fields(gx, gy, lanes):
    def fields(k):
        rows = pl.ds(8 * k, 8)
        x, y = gx[rows, lanes], gy[rows, lanes]
        return [x * x, x * y, y * y]

    return fields


PAIR_LEVEL = (3, 3, 3, 3, 2, 2, 2, 2)


def by_tile(values, shape=(8, LANES)):
    return jnp.where((iota(shape, 1) & 1) == 0, values[0], values[1])


def in_range(lane, start, length):
    return (lane >= start) & (lane < start + length)


def own_exists(mask):
    down = lax.axis_index("tile") < 31
    sec = 2 * lax.axis_index("y") + lax.axis_index("core") < 7
    out = []
    for k, inside in ((1, down), (2, sec)):
        out.append([jnp.where((mask[0, 0, t, k] == 1) & inside, 1.0, 0.0) for t in range(2)])
    return out


def pack_kernel(strips, mask_in, offset_in, bottoms, patches, mask, offset, sems, small_sems):
    small = [pltpu.make_async_copy(mask_in, mask, small_sems.at[0]),
             pltpu.make_async_copy(offset_in, offset, small_sems.at[1])]
    for copy in small:
        copy.start()
    copies = []
    for n, (ref, image) in enumerate(((bottoms, 3), (patches, 4))):
        for t in range(2):
            copies.append(
                pltpu.make_async_copy(strips.at[0, 0, t, image], ref.at[pl.ds(H * t, H)], sems.at[2 * n + t])
            )
    for copy in copies:
        copy.start()
    for copy in small:
        copy.wait()
    exists = own_exists(mask)
    row = iota((8, W), 0)
    for n, ref in enumerate((bottoms, patches)):
        lines = [by_tile(exists[n], (8, W))]
        for d in range(2):
            lines.append(by_tile([offset[0, 0, t, d, n + 1].astype(F32) for t in range(2)], (8, W)))
        block = jnp.where(row == 0, lines[0], jnp.where(row == 1, lines[1], jnp.where(row == 2, lines[2], 0.0)))
        ref[2 * H :, :] = block.astype(jnp.bfloat16)
    for copy in copies:
        copy.wait()


def own_kernel(strips, mask, offset, stiff, out, facts, second, grad, misfit, table, wide, pad):
    kinds = ((1, 0), (3, 3), (4, 4), (2, 2))
    refs = {}
    for kind, images in enumerate(kinds):
        for t in range(2):
            home = grad.at[kind, t] if kind < 2 else second.at[3 - kind, t]
            refs[(kind, t)] = (home.at[0], home.at[1])
            store_gradients(
                lambda lt: strips[0, 0, t, images[t], :, lt * LANES : (lt + 1) * LANES].astype(F32), *refs[(kind, t)], pad
            )
    misfit[...] = strips[0, 0, 0, 1].astype(F32) - strips[0, 0, 1, 0].astype(F32)
    sums = {}
    for lt in range(4):
        lanes = pl.ds(lt * LANES, LANES)
        found = {}
        for kind in range(4):
            for t in range(2):
                got = accumulate(self_fields(*refs[(kind, t)], lanes), (3, 3, 3))
                for n in range(3):
                    found[(3 * kind + n, t)] = got[n]
        for group in range(3):
            put_group(group, lt, {(f, t): found[(4 * group + f, t)] for f in range(4) for t in range(2)}, sums)
        got = accumulate(pair_fields(*refs[(0, 0)], *refs[(0, 1)], misfit, lanes), PAIR_LEVEL)
        right = {(0, 0): got[0], (0, 1): got[1], (1, 0): got[2], (1, 1): got[3],
                 (2, 0): got[4], (3, 0): got[5], (2, 1): got[6], (3, 1): got[7]}
        put_group(3, lt, right, sums)
    out[...] = column_moments(sums, 4, table, wide)
    row = iota((8, LANES), 0)
    lane = iota((8, LANES), 1)
    even = (lane & 1) == 0
    down, sec = own_exists(mask)
    right = jnp.where(mask[0, 0, 0, 0] == 1, 1.0, 0.0)
    pull = in_range(lane, RIGHT + 4, 4)
    factor = jnp.where(lane < 6, right, 0.0)
    factor = jnp.where(in_range(lane, 6, 6), by_tile(down), factor)
    factor = jnp.where(in_range(lane, 12, 6), by_tile(sec), factor)
    factor = jnp.where(in_range(lane, RIGHT, 4), -right, factor)
    factor = jnp.where(pull, jnp.where(even, -2.0, 2.0) * right, factor)
    shift = [offset[0, 0, 0, d, 0].astype(F32) for d in range(2)]
    moved = (~even) & ((lane < 6) | pull)
    lines = [factor]
    lines += [jnp.where(moved, shift[d], 0.0) for d in range(2)]
    lines += [by_tile([stiff[0, 0, t] for t in range(2)])]
    lines += [jnp.full((8, LANES), shift[d], F32) for d in range(2)]
    total = jnp.zeros((8, LANES), F32)
    for n, line in enumerate(lines):
        total = jnp.where(row == n, line, total)
    facts[...] = total


def pair_moments(kind, strips, sent, second, grad, misfit, table, wide, pad):
    for t in range(2):
        rows = pl.ds(H * t, H)
        store_gradients(
            lambda lt: sent[rows, lt * LANES : (lt + 1) * LANES].astype(F32), grad.at[t, 0], grad.at[t, 1], pad
        )
        misfit[t] = sent[rows, :].astype(F32) - strips[0, 0, t, (2, 4)[kind]].astype(F32)
    sums = {}
    for lt in range(4):
        lanes = pl.ds(lt * LANES, LANES)
        cross, pull = {}, {}
        for t in range(2):
            g = [grad.at[t, 0], grad.at[t, 1], second.at[kind, t, 0], second.at[kind, t, 1]]
            got = accumulate(pair_fields(*g, misfit.at[t], lanes), PAIR_LEVEL)
            for n in range(4):
                cross[(n, t)] = got[n]
                pull[(n, t)] = got[4 + n]
        put_group(0, lt, cross, sums)
        put_group(1, lt, pull, sums)
    found = column_moments(sums, 2, table, wide)
    lane = iota((8, LANES), 1)
    moved = jnp.where(in_range(lane, PULL[kind], 8), pltpu.roll(found, PULL[kind] - 8, 1), 0.0)
    return jnp.where(in_range(lane, CROSS[kind], 8), pltpu.roll(found, CROSS[kind], 1), moved)


def down_kernel(strips, upper, second, own, out, grad, misfit, table, wide, pad):
    out[...] = own[...] + pair_moments(0, strips, upper, second, grad, misfit, table, wide, pad)


def sec_kernel(strips, upper, before, second, own, facts, out, grad, misfit, table, wide, pad):
    moments = own[...] + pair_moments(1, strips, before, second, grad, misfit, table, wide, pad)
    lane = iota((1, LANES), 1)
    wide_lane = iota((8, LANES), 1)
    moments = moments + jnp.where(in_range(wide_lane, AGAIN, 6), pltpu.roll(moments, AGAIN - 12, 1), 0.0)
    factor, au, av = facts[0:1, :], facts[1:2, :], facts[2:3, :]
    told = []
    for kind, sent in enumerate((upper, before)):
        known = sent[2 * H :, 0:LANES].astype(F32)
        exists, dx, dy = known[0:1], known[1:2], known[2:3]
        told += [dx, dy]
        alone = in_range(lane, (18, AGAIN)[kind], 6)
        pull_b = in_range(lane, PULL[kind] + 4, 4)
        factor = jnp.where(alone, exists, factor)
        factor = jnp.where(in_range(lane, CROSS[kind], 8), -exists, factor)
        factor = jnp.where(in_range(lane, PULL[kind], 4), -2.0 * exists, factor)
        factor = jnp.where(pull_b, 2.0 * exists, factor)
        au = jnp.where(alone | pull_b, dx, au)
        av = jnp.where(alone | pull_b, dy, av)
    au = au * (1.0 / W)
    av = av * (1.0 / H)
    one, u, v, uu, uv, vv = (moments[n : n + 1, :] for n in range(6))
    lines = [one, u + au * one, v + av * one, uu + 2.0 * au * u + au * au * one,
             uv + au * v + av * u + au * av * one, vv + 2.0 * av * v + av * av * one]
    row = iota((8, LANES), 0)
    full = jnp.zeros((8, LANES), F32)
    for n, line in enumerate(lines):
        full = jnp.where(row == n, line * factor, full)

    def back(x, by):
        return pltpu.roll(x, LANES - by, 1)

    alone = full + back(full, 6) + back(full, 12) + back(full, 18) + back(full, AGAIN)
    alone = pltpu.roll(alone, 58, 1)
    ends = in_range(wide_lane, 58, 2) | in_range(wide_lane, 62, 2)
    alone = jnp.where(ends & ((row == 0) | (row == 3) | (row == 5)), alone + facts[3:4, :], alone)
    load = full + back(full, 24) + back(full, 32)
    final = jnp.where(in_range(wide_lane, 28, 4), load, full)
    final = jnp.where(in_range(wide_lane, 52, 4), back(full, 4), final)
    final = jnp.where(in_range(wide_lane, 58, 6), alone, final)
    tail = (told, [facts[4:5, :], facts[5:6, :]])
    for r in range(2):
        line = jnp.zeros((1, LANES), F32)
        for n, value in enumerate(tail[r]):
            line = jnp.where(in_range(lane, 120 + 2 * n, 2), value, line)
        for n, move in ((2, 56), (1, 16), (0, 104)):
            part = pltpu.roll(final, move, 1)[3 * r + n : 3 * r + n + 1, :]
            line = jnp.where(in_range(lane, 40 * n, 40), part, line)
        out[r : r + 1, :] = line


def solve_kernel(mine, theirs, update_out, residual_out, table):
    core = lax.axis_index("core")
    place = lax.axis_index("y") * 32 + lax.axis_index("tile")
    sub = iota((8, LANES), 0)
    lane = iota((8, LANES), 1)
    c0 = (sub & 1) == 0
    t0 = (sub & 2) == 0
    live = sub < 4
    for r in range(2):
        a = mine[pl.ds(r, LANES, stride=2), :]
        b = theirs[pl.ds(r, LANES, stride=2), :]
        first = jnp.where(core == 0, a, b)
        second = jnp.where(core == 0, b, a)
        table[pl.ds(256 * r, LANES, stride=2), :] = first.T
        table[pl.ds(256 * r + 1, LANES, stride=2), :] = second.T

    def read(r, place):
        return table[pl.ds(256 * r + 4 * place, 8), :]

    def low3(place):
        return read(0, 20 + place), read(0, 40 + place), read(0, place)

    def all6(place):
        return (read(1, place), read(1, 20 + place), read(0, 20 + place), read(1, 40 + place),
                read(0, 40 + place), read(0, place))

    def swap_tile(x):
        return jnp.where(t0, pltpu.roll(x, 6, 0), pltpu.roll(x, 2, 0))

    def swap_core(x):
        return jnp.where(c0, pltpu.roll(x, 7, 0), pltpu.roll(x, 1, 0))

    def row_from_next(x):
        return pltpu.roll(x, LANES - 1, 1)

    def row_to_next(x):
        return pltpu.roll(x, 1, 1)

    def sec_from_next(x):
        x = swap_core(x)
        return jnp.where(c0, x, pltpu.roll(x, LANES - 32, 1))

    def sec_to_next(x):
        x = swap_core(x)
        return jnp.where(c0, pltpu.roll(x, 32, 1), x)

    zero = jnp.zeros((8, LANES), F32)
    du = [read(1, 60) * (1.0 / W), read(0, 60) * (1.0 / W), read(0, 62) * (1.0 / W)]
    dv = [read(1, 61) * (1.0 / H), read(0, 61) * (1.0 / H), read(0, 63) * (1.0 / H)]
    au = jnp.where(t0, zero, du[0])
    av = jnp.where(t0, zero, dv[0])
    bu = jnp.where(t0, du[0], zero)
    bv = jnp.where(t0, dv[0], zero)
    blocks = [all6(17 + n) for n in range(3)]
    square = ((0, 1, 2), (1, 3, 4), (2, 4, 5))
    diagonal = [[blocks[(i // 3) + (j // 3)][square[i % 3][j % 3]] for j in range(6)] for i in range(6)]

    lower = [[None] * 6 for _ in range(6)]
    scaled_col = [[None] * 6 for _ in range(6)]
    inverse_pivot = []
    work = {(i, j): diagonal[i][j] for i in range(6) for j in range(i + 1)}
    for j in range(6):
        inv = 1.0 / work[(j, j)]
        inverse_pivot.append(inv)
        for i in range(j + 1, 6):
            lower[i][j] = work[(i, j)] * inv
        for i in range(j + 1, 6):
            for k in range(j + 1, i + 1):
                work[(i, k)] = work[(i, k)] - lower[i][j] * work[(k, j)]
    inverse = [[None] * 6 for _ in range(6)]
    for j in range(6):
        for i in range(j + 1, 6):
            value = lower[i][j]
            for k in range(j + 1, i):
                value = value + lower[i][k] * inverse[k][j]
            inverse[i][j] = -value

    def precondition(v):
        mid = []
        for i in range(6):
            value = v[i]
            for j in range(i):
                value = value + inverse[i][j] * v[j]
            mid.append(value * inverse_pivot[i])
        out = []
        for i in range(6):
            value = mid[i]
            for j in range(i + 1, 6):
                value = value + inverse[j][i] * mid[j]
            out.append(value)
        return out

    def coupling(m, ra, rb, ca, cb):
        uu, uv, u, vv, v, one = m
        if ra is None:
            return [[uu + ca * u, uv + cb * u, u], [uv + ca * v, vv + cb * v, v], [u + ca * one, v + cb * one, one]]
        return [[uu + (ra + ca) * u, uv + ra * v + cb * u, u + ra * one],
                [uv + ca * v + rb * u, vv + (rb + cb) * v, v + rb * one],
                [u + ca * one, v + cb * one, one]]

    def join(xx, xy, yx, yy):
        return [a + b for a, b in zip(xx, xy)] + [a + b for a, b in zip(yx, yy)]

    down, across = (
        join(*(coupling(all6(place + i), None, None, du[n], dv[n]) for i in range(4))) for n, place in ((1, 4), (2, 8))
    )
    a6, b6 = all6(0), all6(1)
    sa6, sb6 = [swap_tile(x) for x in a6], [swap_tile(x) for x in b6]

    def pick(x, y):
        return [jnp.where(t0, p, q) for p, q in zip(x, y)]

    right = (pick(a6, sa6), pick(sa6, sb6), pick(b6, a6), pick(sb6, b6))
    right = join(*(coupling(m, au, av, bu, bv) for m in right))

    load = []
    for n in range(2):
        for x, y, z in zip(low3(2 + n), low3(12 + n), low3(14 + n)):
            load.append(x + row_from_next(y) + sec_from_next(z))

    def times(block, vector, transpose):
        out = []
        for i in range(6):
            value = None
            for j in range(6):
                term = (block[j][i] if transpose else block[i][j]) * vector[j]
                value = term if value is None else value + term
            out.append(value)
        return out

    down_next = [[row_from_next(x) for x in line] for line in down]
    across_next = [[sec_from_next(x) for x in line] for line in across]

    def multiply(vector):
        parts = [
            times(diagonal, vector, False),
            times(right, [swap_tile(x) for x in vector], False),
            times(down_next, [row_from_next(x) for x in vector], False),
            times(down, [row_to_next(x) for x in vector], True),
            times(across_next, [sec_from_next(x) for x in vector], False),
            times(across, [sec_to_next(x) for x in vector], True),
        ]
        return [functools.reduce(jnp.add, line) for line in zip(*parts)]

    def inner(x, y):
        total = functools.reduce(jnp.add, [a * b for a, b in zip(x, y)])
        total = jnp.where(live, total, 0.0)
        return jnp.sum(total, axis=(0, 1), keepdims=True)

    residual = load
    for step in range(ITERS):
        scaled = precondition(residual)
        image = multiply(scaled)
        rho_next, energy = inner(residual, scaled), inner(scaled, image)
        if step == 0:
            direction, product = scaled, image
            size = rho_next / energy
            update = [size * d for d in direction]
        else:
            ratio = rho_next / rho
            size = rho_next / (energy - ratio * rho_next / size)
            direction = [z + ratio * d for z, d in zip(scaled, direction)]
            product = [z + ratio * d for z, d in zip(image, product)]
            update = [x + size * d for x, d in zip(update, direction)]
        residual = [r - size * p for r, p in zip(residual, product)]
        rho = rho_next

    here = (lane == place) & live & ((sub & 1) == core)
    for vector, out in ((update, update_out), (residual, residual_out)):
        found = zero
        for i in range(6):
            value = jnp.sum(jnp.where(here, vector[i], 0.0), axis=1, keepdims=True)
            found = jnp.where(lane == i, value, found)
        found = found + pltpu.roll(found, 7, 0)
        out[0, 0, 0:1] = found[0:1, :6]
        out[0, 0, 1:2] = found[2:3, :6]


def shards(tile_strips, pair_mask, strip_offset, stiffness):
    tiles = lax.axis_size("tile")
    chips = lax.axis_size("y") * tiles
    sections = lax.axis_size("y") * 2
    offset = jnp.swapaxes(strip_offset, 3, 4)
    image = jax.ShapeDtypeStruct((ROWS, W), tile_strips.dtype)
    bottoms, patches = pl.pallas_call(
        pack_kernel,
        out_shape=(image, image),
        in_specs=[pl.BlockSpec(memory_space=pltpu.HBM)] * 3,
        out_specs=(VMEM, VMEM),
        scratch_shapes=[pltpu.SMEM(pair_mask.shape, jnp.int32), pltpu.SMEM(offset.shape, jnp.int32),
                        pltpu.SemaphoreType.DMA((4,)), pltpu.SemaphoreType.DMA((2,))],
        cost_estimate=pl.CostEstimate(flops=0, bytes_accessed=0, transcendentals=0),
        compiler_params=pltpu.CompilerParams(vmem_limit_bytes=PACK_LIMIT),
        name="pack",
    )(*(pltpu.with_memory_space_constraint(x, pltpu.HBM) for x in (tile_strips, pair_mask, offset)))
    upper = lax.ppermute(bottoms, "tile", [(i, (i + 1) % tiles) for i in range(tiles)])
    before = lax.ppermute(patches, ("y", "core"), [(i, (i + 1) % sections) for i in range(sections)])
    small = jax.ShapeDtypeStruct((8, LANES), F32)
    wide = pltpu.VMEM((8, LANES), F32)
    pad = pltpu.VMEM((4, H + 16, LANES), F32)
    params = pltpu.CompilerParams(vmem_limit_bytes=6 << 20)
    own, facts, second = pl.pallas_call(
        own_kernel,
        out_shape=(small, small, jax.ShapeDtypeStruct((2, 2, 2, H, W), F32)),
        in_specs=[VMEM, SMEM, SMEM, SMEM],
        out_specs=(VMEM, VMEM, VMEM),
        scratch_shapes=[pltpu.VMEM((2, 2, 2, H, W), F32), pltpu.VMEM((H, W), F32), pltpu.VMEM((6, 32, LANES), F32), wide, pad],
        cost_estimate=pl.CostEstimate(flops=20_000_000, bytes_accessed=700_000, transcendentals=0),
        compiler_params=params,
        name="own_moments",
    )(tile_strips, pair_mask, offset, stiffness)
    scratch = [pltpu.VMEM((2, 2, H, W), F32), pltpu.VMEM((2, H, W), F32), pltpu.VMEM((6, 16, LANES), F32), wide, pad]
    cost = pl.CostEstimate(flops=10_000_000, bytes_accessed=900_000, transcendentals=0)
    own = pl.pallas_call(
        down_kernel,
        out_shape=small,
        in_specs=[VMEM] * 4,
        out_specs=VMEM,
        scratch_shapes=scratch,
        cost_estimate=cost,
        compiler_params=params,
        name="down_moments",
    )(tile_strips, upper, second, own)
    message = pl.pallas_call(
        sec_kernel,
        out_shape=jax.ShapeDtypeStruct((2, LANES), F32),
        in_specs=[VMEM] * 6,
        out_specs=VMEM,
        scratch_shapes=scratch,
        cost_estimate=cost,
        compiler_params=params,
        name="sec_moments",
    )(tile_strips, upper, before, second, own, facts)
    sent = jnp.broadcast_to(message[None], (chips, 2, LANES))
    mine = lax.all_to_all(sent, ("y", "tile"), 0, 0)
    theirs = lax.ppermute(mine, "core", [(0, 1), (1, 0)])
    out = jax.ShapeDtypeStruct((1, 1, 2, 6), F32)
    outs = pl.pallas_call(
        solve_kernel,
        out_shape=(out, out),
        in_specs=[VMEM] * 2,
        out_specs=(VMEM, VMEM),
        scratch_shapes=[pltpu.VMEM((2 * 256 + 8, LANES), F32)],
        compiler_params=pltpu.CompilerParams(vmem_limit_bytes=4 << 20),
        name="solve",
    )(mine.reshape(chips * 2, LANES), theirs.reshape(chips * 2, LANES))
    return tuple(jnp.transpose(x, (3, 0, 1, 2)) for x in outs)


def solution(mesh):
    fine = Mesh(mesh.devices.reshape(4, 2, 32), ("y", "core", "tile"))
    sec = ("y", "core")
    return jax.shard_map(
        shards,
        mesh=fine,
        in_specs=(
            P(sec, "tile", None, None, None, None),
            P(sec, "tile", None, None),
            P(sec, "tile", None, None, None),
            P(sec, "tile", None),
        ),
        out_specs=(P(None, sec, "tile", None), P(None, sec, "tile", None)),
        check_vma=False,
    )
```

```python
import functools

import jax
import jax.numpy as jnp
from jax import lax
from jax.experimental import pallas as pl
from jax.experimental.pallas import tpu as pltpu
from jax.sharding import Mesh, PartitionSpec as P


ITERS = 3
H, W = 64, 512
F32 = jnp.float32
LANES = 128
RIGHT, CROSS, PULL, AGAIN = 24, (32, 40), (48, 56), 64
ROWS = 2 * H + 8
SCALE = 2.0**-17

PACK_LIMIT = 2 << 20

VMEM = pl.BlockSpec(memory_space=pltpu.VMEM)
SMEM = pl.BlockSpec(memory_space=pltpu.SMEM)


def iota(shape, axis):
    return lax.broadcasted_iota(jnp.int32, shape, axis)


def store_gradients(image, gx_ref, gy_ref, pad):
    lane = iota((8, LANES), 1)
    inner_first, inner_last = lane > 0, lane < LANES - 1
    zero = jnp.zeros((8, LANES), F32)
    tiles = []
    for lt in range(4):
        x = image(lt)
        pad[lt, 0:8] = zero
        pad[lt, 8 : 8 + H] = x
        pad[lt, 8 + H : 16 + H] = zero
        tiles.append([x[8 * k : 8 * k + 8] for k in range(8)])
    for k in range(8):
        ahead = [pltpu.roll(tiles[lt][k], LANES - 1, 1) for lt in range(4)] + [zero]
        behind = [zero] + [pltpu.roll(tiles[lt][k], 1, 1) for lt in range(4)]
        for lt in range(4):
            here = pl.ds(8 * k, 8), pl.ds(lt * LANES, LANES)
            gx_ref[here] = jnp.where(inner_last, ahead[lt], ahead[lt + 1]) - jnp.where(
                inner_first, behind[lt + 1], behind[lt]
            )
            gy_ref[here] = pad[lt, 9 + 8 * k : 17 + 8 * k] - pad[lt, 7 + 8 * k : 15 + 8 * k]


def row_moments(sums, level):
    c = 0.5 + iota((8, LANES), 0).astype(F32) / H
    out = [sums[0], c * sums[0] - sums[1] * 0.125]
    if level == 3:
        out.append((c * c) * sums[0] - (0.25 * c + 1.0 / 64.0) * sums[1] + sums[2] * (1.0 / 32.0))
    return out


def accumulate(fields, level):
    sums = None
    for k in range(8):
        values = fields(k)
        if sums is None:
            sums = [[v] * lv for v, lv in zip(values, level)]
            continue
        new = []
        for v, old, lv in zip(values, sums, level):
            now = [old[0] + v]
            for q in range(1, lv):
                now.append(old[q] + now[q - 1])
            new.append(now)
        sums = new
    return [row_moments(s, lv) for s, lv in zip(sums, level)]


def tree8(vs):
    s = iota((8, LANES), 0)
    m4 = s < 4
    w = []
    for i in range(4):
        x = jnp.where(m4, vs[i], vs[i + 4])
        y = jnp.where(m4, vs[i + 4], vs[i])
        w.append(x + pltpu.roll(y, 4, 0))
    m2 = (s & 2) == 0
    z = []
    for i in range(2):
        x = jnp.where(m2, w[i], w[i + 2])
        y = jnp.where(m2, w[i + 2], w[i])
        z.append(x + jnp.where(m2, pltpu.roll(y, 6, 0), pltpu.roll(y, 2, 0)))
    m1 = (s & 1) == 0
    x = jnp.where(m1, z[0], z[1])
    y = jnp.where(m1, z[1], z[0])
    return x + jnp.where(m1, pltpu.roll(y, 7, 0), pltpu.roll(y, 1, 0))


def put_group(group, lt, found, total):
    order = [found[(f, t)] for f in range(4) for t in range(2)]
    low = [tree8([v[q] for v in order]) for q in range(2)]
    u = (iota((8, LANES), 1) + lt * LANES).astype(F32) / W - 0.5
    new = [low[0], u * low[0], low[1]]
    if any(len(v) > 2 for v in order):
        zero = jnp.zeros((8, LANES), F32)
        new += [(u * u) * low[0], u * low[1], tree8([v[2] if len(v) > 2 else zero for v in order])]
    for m, value in enumerate(new):
        total[(m, group)] = total[(m, group)] + value if lt else value


def column_moments(total, groups, table, wide):
    dims = (((1,), (1,)), ((), ()))
    zero = jnp.zeros((8, LANES), F32)
    scale = jnp.full((8, LANES), SCALE, F32)
    row = iota((8, 8 * groups), 0)
    out = None
    for m in range(6):
        for group in range(groups):
            table[m, pl.ds(8 * group, 8)] = total.get((m, group), zero)
        part = lax.dot_general(
            scale, table[m], dims, precision=lax.Precision.HIGHEST, preferred_element_type=F32
        )
        out = part if out is None else jnp.where(row == m, part, out)
    wide[...] = zero
    wide[0:6, 0 : 8 * groups] = out[0:6]
    return wide[...]


def pair_fields(gxa, gya, gxb, gyb, misfit, lanes):
    def fields(k):
        rows = pl.ds(8 * k, 8)
        xa, ya, xb, yb, m = (ref[rows, lanes] for ref in (gxa, gya, gxb, gyb, misfit))
        return [xa * xb, xa * yb, ya * xb, ya * yb, xa * m, ya * m, xb * m, yb * m]

    return fields


def self_fields(gx, gy, lanes):
    def fields(k):
        rows = pl.ds(8 * k, 8)
        x, y = gx[rows, lanes], gy[rows, lanes]
        return [x * x, x * y, y * y]

    return fields


PAIR_LEVEL = (3, 3, 3, 3, 2, 2, 2, 2)


def by_tile(values, shape=(8, LANES)):
    return jnp.where((iota(shape, 1) & 1) == 0, values[0], values[1])


def in_range(lane, start, length):
    return (lane >= start) & (lane < start + length)


def own_exists(mask):
    down = lax.axis_index("tile") < 31
    sec = 2 * lax.axis_index("y") + lax.axis_index("core") < 7
    out = []
    for k, inside in ((1, down), (2, sec)):
        out.append([jnp.where((mask[0, 0, t, k] == 1) & inside, 1.0, 0.0) for t in range(2)])
    return out


def pack_kernel(strips, mask_in, offset_in, bottoms, patches, mask, offset, sems, small_sems):
    small = [pltpu.make_async_copy(mask_in, mask, small_sems.at[0]),
             pltpu.make_async_copy(offset_in, offset, small_sems.at[1])]
    for copy in small:
        copy.start()
    copies = []
    for n, (ref, image) in enumerate(((bottoms, 3), (patches, 4))):
        for t in range(2):
            copies.append(
                pltpu.make_async_copy(strips.at[0, 0, t, image], ref.at[pl.ds(H * t, H)], sems.at[2 * n + t])
            )
    for copy in copies:
        copy.start()
    for copy in small:
        copy.wait()
    exists = own_exists(mask)
    row = iota((8, W), 0)
    for n, ref in enumerate((bottoms, patches)):
        lines = [by_tile(exists[n], (8, W))]
        for d in range(2):
            lines.append(by_tile([offset[0, 0, t, d, n + 1].astype(F32) for t in range(2)], (8, W)))
        block = jnp.where(row == 0, lines[0], jnp.where(row == 1, lines[1], jnp.where(row == 2, lines[2], 0.0)))
        ref[2 * H :, :] = block.astype(jnp.bfloat16)
    for copy in copies:
        copy.wait()


def own_kernel(strips, mask, offset, stiff, out, facts, second, grad, misfit, table, wide, pad):
    kinds = ((1, 0), (3, 3), (4, 4), (2, 2))
    refs = {}
    for kind, images in enumerate(kinds):
        for t in range(2):
            home = grad.at[kind, t] if kind < 2 else second.at[3 - kind, t]
            refs[(kind, t)] = (home.at[0], home.at[1])
            store_gradients(
                lambda lt: strips[0, 0, t, images[t], :, lt * LANES : (lt + 1) * LANES].astype(F32), *refs[(kind, t)], pad
            )
    misfit[...] = strips[0, 0, 0, 1].astype(F32) - strips[0, 0, 1, 0].astype(F32)
    sums = {}
    for lt in range(4):
        lanes = pl.ds(lt * LANES, LANES)
        found = {}
        for kind in range(4):
            for t in range(2):
                got = accumulate(self_fields(*refs[(kind, t)], lanes), (3, 3, 3))
                for n in range(3):
                    found[(3 * kind + n, t)] = got[n]
        for group in range(3):
            put_group(group, lt, {(f, t): found[(4 * group + f, t)] for f in range(4) for t in range(2)}, sums)
        got = accumulate(pair_fields(*refs[(0, 0)], *refs[(0, 1)], misfit, lanes), PAIR_LEVEL)
        right = {(0, 0): got[0], (0, 1): got[1], (1, 0): got[2], (1, 1): got[3],
                 (2, 0): got[4], (3, 0): got[5], (2, 1): got[6], (3, 1): got[7]}
        put_group(3, lt, right, sums)
    out[...] = column_moments(sums, 4, table, wide)
    row = iota((8, LANES), 0)
    lane = iota((8, LANES), 1)
    even = (lane & 1) == 0
    down, sec = own_exists(mask)
    right = jnp.where(mask[0, 0, 0, 0] == 1, 1.0, 0.0)
    pull = in_range(lane, RIGHT + 4, 4)
    factor = jnp.where(lane < 6, right, 0.0)
    factor = jnp.where(in_range(lane, 6, 6), by_tile(down), factor)
    factor = jnp.where(in_range(lane, 12, 6), by_tile(sec), factor)
    factor = jnp.where(in_range(lane, RIGHT, 4), -right, factor)
    factor = jnp.where(pull, jnp.where(even, -2.0, 2.0) * right, factor)
    shift = [offset[0, 0, 0, d, 0].astype(F32) for d in range(2)]
    moved = (~even) & ((lane < 6) | pull)
    lines = [factor]
    lines += [jnp.where(moved, shift[d], 0.0) for d in range(2)]
    lines += [by_tile([stiff[0, 0, t] for t in range(2)])]
    lines += [jnp.full((8, LANES), shift[d], F32) for d in range(2)]
    total = jnp.zeros((8, LANES), F32)
    for n, line in enumerate(lines):
        total = jnp.where(row == n, line, total)
    facts[...] = total


def pair_moments(kind, strips, sent, second, grad, misfit, pad):
    for t in range(2):
        rows = pl.ds(H * t, H)
        store_gradients(
            lambda lt: sent[rows, lt * LANES : (lt + 1) * LANES].astype(F32), grad.at[t, 0], grad.at[t, 1], pad
        )
        misfit[t] = sent[rows, :].astype(F32) - strips[0, 0, t, (2, 4)[kind]].astype(F32)
    sums = {}
    for lt in range(4):
        lanes = pl.ds(lt * LANES, LANES)
        cross, pull = {}, {}
        for t in range(2):
            g = [grad.at[t, 0], grad.at[t, 1], second.at[kind, t, 0], second.at[kind, t, 1]]
            got = accumulate(pair_fields(*g, misfit.at[t], lanes), PAIR_LEVEL)
            for n in range(4):
                cross[(n, t)] = got[n]
                pull[(n, t)] = got[4 + n]
        put_group(0, lt, cross, sums)
        put_group(1, lt, pull, sums)
    return sums


def sec_kernel(strips, before, second, out, grad, misfit, pad):
    sums = pair_moments(1, strips, before, second, grad, misfit, pad)
    for m in range(6):
        for group in range(2):
            out[m, pl.ds(8 * group, 8)] = sums.get((m, group), jnp.zeros((8, LANES), F32))


def down_kernel(strips, upper, before, second, own, facts, sec, out, grad, misfit, pad, table, wide):
    sums = pair_moments(0, strips, upper, second, grad, misfit, pad)
    for m in range(6):
        for group in range(2):
            sums[(m, 2 + group)] = sec[m, pl.ds(8 * group, 8)]
    found = column_moments(sums, 4, table, wide)
    to = iota((8, LANES), 1)
    moments = own[...] + jnp.where(
        in_range(to, 40, 8),
        pltpu.roll(found, 24, 1),
        jnp.where(in_range(to, 48, 8), pltpu.roll(found, 40, 1), jnp.where(in_range(to, 32, 32), pltpu.roll(found, 32, 1), 0.0)),
    )
    lane = iota((1, LANES), 1)
    wide_lane = iota((8, LANES), 1)
    moments = moments + jnp.where(in_range(wide_lane, AGAIN, 6), pltpu.roll(moments, AGAIN - 12, 1), 0.0)
    factor, au, av = facts[0:1, :], facts[1:2, :], facts[2:3, :]
    told = []
    for kind, sent in enumerate((upper, before)):
        known = sent[2 * H :, 0:LANES].astype(F32)
        exists, dx, dy = known[0:1], known[1:2], known[2:3]
        told += [dx, dy]
        alone = in_range(lane, (18, AGAIN)[kind], 6)
        pull_b = in_range(lane, PULL[kind] + 4, 4)
        factor = jnp.where(alone, exists, factor)
        factor = jnp.where(in_range(lane, CROSS[kind], 8), -exists, factor)
        factor = jnp.where(in_range(lane, PULL[kind], 4), -2.0 * exists, factor)
        factor = jnp.where(pull_b, 2.0 * exists, factor)
        au = jnp.where(alone | pull_b, dx, au)
        av = jnp.where(alone | pull_b, dy, av)
    au = au * (1.0 / W)
    av = av * (1.0 / H)
    one, u, v, uu, uv, vv = (moments[n : n + 1, :] for n in range(6))
    lines = [one, u + au * one, v + av * one, uu + 2.0 * au * u + au * au * one,
             uv + au * v + av * u + au * av * one, vv + 2.0 * av * v + av * av * one]
    row = iota((8, LANES), 0)
    full = jnp.zeros((8, LANES), F32)
    for n, line in enumerate(lines):
        full = jnp.where(row == n, line * factor, full)

    def back(x, by):
        return pltpu.roll(x, LANES - by, 1)

    alone = full + back(full, 6) + back(full, 12) + back(full, 18) + back(full, AGAIN)
    alone = pltpu.roll(alone, 58, 1)
    ends = in_range(wide_lane, 58, 2) | in_range(wide_lane, 62, 2)
    alone = jnp.where(ends & ((row == 0) | (row == 3) | (row == 5)), alone + facts[3:4, :], alone)
    load = full + back(full, 24) + back(full, 32)
    final = jnp.where(in_range(wide_lane, 28, 4), load, full)
    final = jnp.where(in_range(wide_lane, 52, 4), back(full, 4), final)
    final = jnp.where(in_range(wide_lane, 58, 6), alone, final)
    tail = (told, [facts[4:5, :], facts[5:6, :]])
    for r in range(2):
        line = jnp.zeros((1, LANES), F32)
        for n, value in enumerate(tail[r]):
            line = jnp.where(in_range(lane, 120 + 2 * n, 2), value, line)
        for n, move in ((2, 56), (1, 16), (0, 104)):
            part = pltpu.roll(final, move, 1)[3 * r + n : 3 * r + n + 1, :]
            line = jnp.where(in_range(lane, 40 * n, 40), part, line)
        out[r : r + 1, :] = line


def solve_kernel(mine, theirs, update_out, residual_out, table):
    core = lax.axis_index("core")
    place = lax.axis_index("y") * 32 + lax.axis_index("tile")
    sub = iota((8, LANES), 0)
    lane = iota((8, LANES), 1)
    c0 = (sub & 1) == 0
    t0 = (sub & 2) == 0
    live = sub < 4
    for r in range(2):
        a = mine[pl.ds(r, LANES, stride=2), :]
        b = theirs[pl.ds(r, LANES, stride=2), :]
        first = jnp.where(core == 0, a, b)
        second = jnp.where(core == 0, b, a)
        table[pl.ds(256 * r, LANES, stride=2), :] = first.T
        table[pl.ds(256 * r + 1, LANES, stride=2), :] = second.T

    def read(r, place):
        return table[pl.ds(256 * r + 4 * place, 8), :]

    def low3(place):
        return read(0, 20 + place), read(0, 40 + place), read(0, place)

    def all6(place):
        return (read(1, place), read(1, 20 + place), read(0, 20 + place), read(1, 40 + place),
                read(0, 40 + place), read(0, place))

    def swap_tile(x):
        return jnp.where(t0, pltpu.roll(x, 6, 0), pltpu.roll(x, 2, 0))

    def swap_core(x):
        return jnp.where(c0, pltpu.roll(x, 7, 0), pltpu.roll(x, 1, 0))

    def row_from_next(x):
        return pltpu.roll(x, LANES - 1, 1)

    def row_to_next(x):
        return pltpu.roll(x, 1, 1)

    def sec_from_next(x):
        x = swap_core(x)
        return jnp.where(c0, x, pltpu.roll(x, LANES - 32, 1))

    def sec_to_next(x):
        x = swap_core(x)
        return jnp.where(c0, pltpu.roll(x, 32, 1), x)

    zero = jnp.zeros((8, LANES), F32)
    du = [read(1, 60) * (1.0 / W), read(0, 60) * (1.0 / W), read(0, 62) * (1.0 / W)]
    dv = [read(1, 61) * (1.0 / H), read(0, 61) * (1.0 / H), read(0, 63) * (1.0 / H)]
    au = jnp.where(t0, zero, du[0])
    av = jnp.where(t0, zero, dv[0])
    bu = jnp.where(t0, du[0], zero)
    bv = jnp.where(t0, dv[0], zero)
    blocks = [all6(17 + n) for n in range(3)]
    square = ((0, 1, 2), (1, 3, 4), (2, 4, 5))
    diagonal = [[blocks[(i // 3) + (j // 3)][square[i % 3][j % 3]] for j in range(6)] for i in range(6)]

    lower = [[None] * 6 for _ in range(6)]
    inverse_pivot = []
    work = {(i, j): diagonal[i][j] for i in range(6) for j in range(i + 1)}
    for j in range(6):
        inv = 1.0 / work[(j, j)]
        inverse_pivot.append(inv)
        for i in range(j + 1, 6):
            lower[i][j] = work[(i, j)] * inv
        for i in range(j + 1, 6):
            for k in range(j + 1, i + 1):
                work[(i, k)] = work[(i, k)] - lower[i][j] * work[(k, j)]
    inverse = [[None] * 6 for _ in range(6)]
    for j in range(6):
        for i in range(j + 1, 6):
            value = lower[i][j]
            for k in range(j + 1, i):
                value = value + lower[i][k] * inverse[k][j]
            inverse[i][j] = -value

    def precondition(v):
        mid = []
        for i in range(6):
            value = v[i]
            for j in range(i):
                value = value + inverse[i][j] * v[j]
            mid.append(value * inverse_pivot[i])
        out = []
        for i in range(6):
            value = mid[i]
            for j in range(i + 1, 6):
                value = value + inverse[j][i] * mid[j]
            out.append(value)
        return out

    def coupling(m, ra, rb, ca, cb):
        uu, uv, u, vv, v, one = m
        if ra is None:
            return [[uu + ca * u, uv + cb * u, u], [uv + ca * v, vv + cb * v, v], [u + ca * one, v + cb * one, one]]
        return [[uu + (ra + ca) * u, uv + ra * v + cb * u, u + ra * one],
                [uv + ca * v + rb * u, vv + (rb + cb) * v, v + rb * one],
                [u + ca * one, v + cb * one, one]]

    def join(xx, xy, yx, yy):
        return [a + b for a, b in zip(xx, xy)] + [a + b for a, b in zip(yx, yy)]

    down, across = (
        join(*(coupling(all6(place + i), None, None, du[n], dv[n]) for i in range(4))) for n, place in ((1, 4), (2, 8))
    )
    a6, b6 = all6(0), all6(1)
    sa6, sb6 = [swap_tile(x) for x in a6], [swap_tile(x) for x in b6]

    def pick(x, y):
        return [jnp.where(t0, p, q) for p, q in zip(x, y)]

    right = (pick(a6, sa6), pick(sa6, sb6), pick(b6, a6), pick(sb6, b6))
    right = join(*(coupling(m, au, av, bu, bv) for m in right))

    load = []
    for n in range(2):
        for x, y, z in zip(low3(2 + n), low3(12 + n), low3(14 + n)):
            load.append(x + row_from_next(y) + sec_from_next(z))

    def times(block, vector, transpose):
        out = []
        for i in range(6):
            value = None
            for j in range(6):
                term = (block[j][i] if transpose else block[i][j]) * vector[j]
                value = term if value is None else value + term
            out.append(value)
        return out

    down_next = [[row_from_next(x) for x in line] for line in down]
    across_next = [[sec_from_next(x) for x in line] for line in across]

    def multiply(vector):
        parts = [
            times(diagonal, vector, False),
            times(right, [swap_tile(x) for x in vector], False),
            times(down_next, [row_from_next(x) for x in vector], False),
            times(down, [row_to_next(x) for x in vector], True),
            times(across_next, [sec_from_next(x) for x in vector], False),
            times(across, [sec_to_next(x) for x in vector], True),
        ]
        return [functools.reduce(jnp.add, line) for line in zip(*parts)]

    def inner(x, y):
        total = functools.reduce(jnp.add, [a * b for a, b in zip(x, y)])
        total = jnp.where(live, total, 0.0)
        return jnp.sum(total, axis=(0, 1), keepdims=True)

    residual = load
    for step in range(ITERS):
        scaled = precondition(residual)
        image = multiply(scaled)
        rho_next, energy = inner(residual, scaled), inner(scaled, image)
        if step == 0:
            direction, product = scaled, image
            size = rho_next / energy
            update = [size * d for d in direction]
        else:
            ratio = rho_next / rho
            size = rho_next / (energy - ratio * rho_next / size)
            direction = [z + ratio * d for z, d in zip(scaled, direction)]
            product = [z + ratio * d for z, d in zip(image, product)]
            update = [x + size * d for x, d in zip(update, direction)]
        residual = [r - size * p for r, p in zip(residual, product)]
        rho = rho_next

    here = (lane == place) & live & ((sub & 1) == core)
    for vector, out in ((update, update_out), (residual, residual_out)):
        found = zero
        for i in range(6):
            value = jnp.sum(jnp.where(here, vector[i], 0.0), axis=1, keepdims=True)
            found = jnp.where(lane == i, value, found)
        found = found + pltpu.roll(found, 7, 0)
        out[0, 0, 0:1] = found[0:1, :6]
        out[0, 0, 1:2] = found[2:3, :6]


def shards(tile_strips, pair_mask, strip_offset, stiffness):
    tiles = lax.axis_size("tile")
    chips = lax.axis_size("y") * tiles
    sections = lax.axis_size("y") * 2
    offset = jnp.swapaxes(strip_offset, 3, 4)
    image = jax.ShapeDtypeStruct((ROWS, W), tile_strips.dtype)
    bottoms, patches = pl.pallas_call(
        pack_kernel,
        out_shape=(image, image),
        in_specs=[pl.BlockSpec(memory_space=pltpu.HBM)] * 3,
        out_specs=(VMEM, VMEM),
        scratch_shapes=[pltpu.SMEM(pair_mask.shape, jnp.int32), pltpu.SMEM(offset.shape, jnp.int32),
                        pltpu.SemaphoreType.DMA((4,)), pltpu.SemaphoreType.DMA((2,))],
        cost_estimate=pl.CostEstimate(flops=0, bytes_accessed=0, transcendentals=0),
        compiler_params=pltpu.CompilerParams(vmem_limit_bytes=PACK_LIMIT),
        name="pack",
    )(*(pltpu.with_memory_space_constraint(x, pltpu.HBM) for x in (tile_strips, pair_mask, offset)))
    upper = lax.ppermute(bottoms, "tile", [(i, (i + 1) % tiles) for i in range(tiles)])
    before = lax.ppermute(patches, ("y", "core"), [(i, (i + 1) % sections) for i in range(sections)])
    small = jax.ShapeDtypeStruct((8, LANES), F32)
    wide = pltpu.VMEM((8, LANES), F32)
    pad = pltpu.VMEM((4, H + 16, LANES), F32)
    params = pltpu.CompilerParams(vmem_limit_bytes=6 << 20)
    own, facts, second = pl.pallas_call(
        own_kernel,
        out_shape=(small, small, jax.ShapeDtypeStruct((2, 2, 2, H, W), F32)),
        in_specs=[VMEM, SMEM, SMEM, SMEM],
        out_specs=(VMEM, VMEM, VMEM),
        scratch_shapes=[pltpu.VMEM((2, 2, 2, H, W), F32), pltpu.VMEM((H, W), F32), pltpu.VMEM((6, 32, LANES), F32), wide, pad],
        cost_estimate=pl.CostEstimate(flops=20_000_000, bytes_accessed=700_000, transcendentals=0),
        compiler_params=params,
        name="own_moments",
    )(tile_strips, pair_mask, offset, stiffness)
    scratch = [pltpu.VMEM((2, 2, H, W), F32), pltpu.VMEM((2, H, W), F32), pad]
    cost = pl.CostEstimate(flops=10_000_000, bytes_accessed=900_000, transcendentals=0)
    sec = pl.pallas_call(
        sec_kernel,
        out_shape=jax.ShapeDtypeStruct((6, 16, LANES), F32),
        in_specs=[VMEM] * 3,
        out_specs=VMEM,
        scratch_shapes=scratch,
        cost_estimate=cost,
        compiler_params=params,
        name="sec_moments",
    )(tile_strips, before, second)
    message = pl.pallas_call(
        down_kernel,
        out_shape=jax.ShapeDtypeStruct((2, LANES), F32),
        in_specs=[VMEM] * 7,
        out_specs=VMEM,
        scratch_shapes=[*scratch, pltpu.VMEM((6, 32, LANES), F32), wide],
        cost_estimate=cost,
        compiler_params=params,
        name="down_moments",
    )(tile_strips, upper, before, second, own, facts, sec)
    sent = jnp.broadcast_to(message[None], (chips, 2, LANES))
    mine = lax.all_to_all(sent, ("y", "tile"), 0, 0)
    theirs = lax.ppermute(mine, "core", [(0, 1), (1, 0)])
    out = jax.ShapeDtypeStruct((1, 1, 2, 6), F32)
    outs = pl.pallas_call(
        solve_kernel,
        out_shape=(out, out),
        in_specs=[VMEM] * 2,
        out_specs=(VMEM, VMEM),
        scratch_shapes=[pltpu.VMEM((2 * 256 + 8, LANES), F32)],
        compiler_params=pltpu.CompilerParams(vmem_limit_bytes=4 << 20),
        name="solve",
    )(mine.reshape(chips * 2, LANES), theirs.reshape(chips * 2, LANES))
    return tuple(jnp.transpose(x, (3, 0, 1, 2)) for x in outs)


def solution(mesh):
    fine = Mesh(mesh.devices.reshape(4, 2, 32), ("y", "core", "tile"))
    sec = ("y", "core")
    return jax.shard_map(
        shards,
        mesh=fine,
        in_specs=(
            P(sec, "tile", None, None, None, None),
            P(sec, "tile", None, None),
            P(sec, "tile", None, None, None),
            P(sec, "tile", None),
        ),
        out_specs=(P(None, sec, "tile", None), P(None, sec, "tile", None)),
        check_vma=False,
    )
```

```python
import functools

import jax
import jax.numpy as jnp
from jax import lax
from jax.experimental import pallas as pl
from jax.experimental.pallas import tpu as pltpu
from jax.sharding import Mesh, PartitionSpec as P


ITERS = 3
H, W = 64, 512
F32 = jnp.float32
LANES = 128
RIGHT, CROSS, PULL, AGAIN = 24, (32, 40), (48, 56), 64
ROWS = 2 * H + 8
SCALE = 2.0**-17

PACK_LIMIT = 2 << 20

VMEM = pl.BlockSpec(memory_space=pltpu.VMEM)
SMEM = pl.BlockSpec(memory_space=pltpu.SMEM)


def iota(shape, axis):
    return lax.broadcasted_iota(jnp.int32, shape, axis)


def store_gradients(image, gx_ref, gy_ref, pad):
    lane = iota((8, LANES), 1)
    inner_first, inner_last = lane > 0, lane < LANES - 1
    zero = jnp.zeros((8, LANES), F32)
    tiles = []
    for lt in range(4):
        x = image(lt)
        pad[lt, 0:8] = zero
        pad[lt, 8 : 8 + H] = x
        pad[lt, 8 + H : 16 + H] = zero
        tiles.append([x[8 * k : 8 * k + 8] for k in range(8)])
    for k in range(8):
        ahead = [pltpu.roll(tiles[lt][k], LANES - 1, 1) for lt in range(4)] + [zero]
        behind = [zero] + [pltpu.roll(tiles[lt][k], 1, 1) for lt in range(4)]
        for lt in range(4):
            here = pl.ds(8 * k, 8), pl.ds(lt * LANES, LANES)
            gx_ref[here] = jnp.where(inner_last, ahead[lt], ahead[lt + 1]) - jnp.where(
                inner_first, behind[lt + 1], behind[lt]
            )
            gy_ref[here] = pad[lt, 9 + 8 * k : 17 + 8 * k] - pad[lt, 7 + 8 * k : 15 + 8 * k]


def row_moments(sums, level):
    c = 0.5 + iota((8, LANES), 0).astype(F32) / H
    out = [sums[0], c * sums[0] - sums[1] * 0.125]
    if level == 3:
        out.append((c * c) * sums[0] - (0.25 * c + 1.0 / 64.0) * sums[1] + sums[2] * (1.0 / 32.0))
    return out


def accumulate(fields, level):
    sums = None
    for k in range(8):
        values = fields(k)
        if sums is None:
            sums = [[v] * lv for v, lv in zip(values, level)]
            continue
        new = []
        for v, old, lv in zip(values, sums, level):
            now = [old[0] + v]
            for q in range(1, lv):
                now.append(old[q] + now[q - 1])
            new.append(now)
        sums = new
    return [row_moments(s, lv) for s, lv in zip(sums, level)]


def tree8(vs):
    s = iota((8, LANES), 0)
    m4 = s < 4
    w = []
    for i in range(4):
        x = jnp.where(m4, vs[i], vs[i + 4])
        y = jnp.where(m4, vs[i + 4], vs[i])
        w.append(x + pltpu.roll(y, 4, 0))
    m2 = (s & 2) == 0
    z = []
    for i in range(2):
        x = jnp.where(m2, w[i], w[i + 2])
        y = jnp.where(m2, w[i + 2], w[i])
        z.append(x + jnp.where(m2, pltpu.roll(y, 6, 0), pltpu.roll(y, 2, 0)))
    m1 = (s & 1) == 0
    x = jnp.where(m1, z[0], z[1])
    y = jnp.where(m1, z[1], z[0])
    return x + jnp.where(m1, pltpu.roll(y, 7, 0), pltpu.roll(y, 1, 0))


def put_group(group, lt, found, total):
    order = [found[(f, t)] for f in range(4) for t in range(2)]
    low = [tree8([v[q] for v in order]) for q in range(2)]
    u = (iota((8, LANES), 1) + lt * LANES).astype(F32) / W - 0.5
    new = [low[0], u * low[0], low[1]]
    if any(len(v) > 2 for v in order):
        zero = jnp.zeros((8, LANES), F32)
        new += [(u * u) * low[0], u * low[1], tree8([v[2] if len(v) > 2 else zero for v in order])]
    for m, value in enumerate(new):
        total[(m, group)] = total[(m, group)] + value if lt else value


def column_moments(total, groups, table, wide, start=0):
    dims = (((1,), (1,)), ((), ()))
    zero = jnp.zeros((8, LANES), F32)
    scale = jnp.full((8, LANES), SCALE, F32)
    row = iota((8, 8 * groups), 0)
    out = None
    for m in range(6):
        for group in range(groups):
            table[m, pl.ds(8 * group, 8)] = total.get((m, group), zero)
        part = lax.dot_general(
            scale, table[m], dims, precision=lax.Precision.HIGHEST, preferred_element_type=F32
        )
        out = part if out is None else jnp.where(row == m, part, out)
    wide[...] = zero
    wide[0:6, start : start + 8 * groups] = out[0:6]
    return wide[...]


def pair_fields(gxa, gya, gxb, gyb, misfit, lanes):
    def fields(k):
        rows = pl.ds(8 * k, 8)
        xa, ya, xb, yb, m = (ref[rows, lanes] for ref in (gxa, gya, gxb, gyb, misfit))
        return [xa * xb, xa * yb, ya * xb, ya * yb, xa * m, ya * m, xb * m, yb * m]

    return fields


def self_fields(gx, gy, lanes):
    def fields(k):
        rows = pl.ds(8 * k, 8)
        x, y = gx[rows, lanes], gy[rows, lanes]
        return [x * x, x * y, y * y]

    return fields


PAIR_LEVEL = (3, 3, 3, 3, 2, 2, 2, 2)


def by_tile(values, shape=(8, LANES)):
    return jnp.where((iota(shape, 1) & 1) == 0, values[0], values[1])


def in_range(lane, start, length):
    return (lane >= start) & (lane < start + length)


def own_exists(mask):
    down = lax.axis_index("tile") < 31
    sec = 2 * lax.axis_index("y") + lax.axis_index("core") < 7
    out = []
    for k, inside in ((1, down), (2, sec)):
        out.append([jnp.where((mask[0, 0, t, k] == 1) & inside, 1.0, 0.0) for t in range(2)])
    return out


def pack_kernel(strips, mask_in, offset_in, bottoms, patches, mask, offset, sems, small_sems):
    small = [pltpu.make_async_copy(mask_in, mask, small_sems.at[0]),
             pltpu.make_async_copy(offset_in, offset, small_sems.at[1])]
    for copy in small:
        copy.start()
    copies = []
    for n, (ref, image) in enumerate(((bottoms, 3), (patches, 4))):
        for t in range(2):
            copies.append(
                pltpu.make_async_copy(strips.at[0, 0, t, image], ref.at[pl.ds(H * t, H)], sems.at[2 * n + t])
            )
    for copy in copies:
        copy.start()
    for copy in small:
        copy.wait()
    exists = own_exists(mask)
    row = iota((8, W), 0)
    for n, ref in enumerate((bottoms, patches)):
        lines = [by_tile(exists[n], (8, W))]
        for d in range(2):
            lines.append(by_tile([offset[0, 0, t, d, n + 1].astype(F32) for t in range(2)], (8, W)))
        block = jnp.where(row == 0, lines[0], jnp.where(row == 1, lines[1], jnp.where(row == 2, lines[2], 0.0)))
        ref[2 * H :, :] = block.astype(jnp.bfloat16)
    for copy in copies:
        copy.wait()


def own_kernel(strips, mask, offset, stiff, out, facts, second, grad, misfit, table, wide, pad):
    kinds = ((1, 0), (3, 3), (4, 4), (2, 2))
    refs = {}
    for kind, images in enumerate(kinds):
        for t in range(2):
            home = grad.at[kind, t] if kind < 2 else second.at[3 - kind, t]
            refs[(kind, t)] = (home.at[0], home.at[1])
            store_gradients(
                lambda lt: strips[0, 0, t, images[t], :, lt * LANES : (lt + 1) * LANES].astype(F32), *refs[(kind, t)], pad
            )
    misfit[...] = strips[0, 0, 0, 1].astype(F32) - strips[0, 0, 1, 0].astype(F32)
    sums = {}
    for lt in range(4):
        lanes = pl.ds(lt * LANES, LANES)
        found = {}
        for kind in range(4):
            for t in range(2):
                got = accumulate(self_fields(*refs[(kind, t)], lanes), (3, 3, 3))
                for n in range(3):
                    found[(3 * kind + n, t)] = got[n]
        for group in range(3):
            put_group(group, lt, {(f, t): found[(4 * group + f, t)] for f in range(4) for t in range(2)}, sums)
        got = accumulate(pair_fields(*refs[(0, 0)], *refs[(0, 1)], misfit, lanes), PAIR_LEVEL)
        right = {(0, 0): got[0], (0, 1): got[1], (1, 0): got[2], (1, 1): got[3],
                 (2, 0): got[4], (3, 0): got[5], (2, 1): got[6], (3, 1): got[7]}
        put_group(3, lt, right, sums)
    found = column_moments(sums, 4, table, wide)
    row = iota((8, LANES), 0)
    lane = iota((8, LANES), 1)
    out[...] = found + jnp.where(in_range(lane, AGAIN, 6), pltpu.roll(found, AGAIN - 12, 1), 0.0)
    even = (lane & 1) == 0
    down, sec = own_exists(mask)
    right = jnp.where(mask[0, 0, 0, 0] == 1, 1.0, 0.0)
    pull = in_range(lane, RIGHT + 4, 4)
    factor = jnp.where(lane < 6, right, 0.0)
    factor = jnp.where(in_range(lane, 6, 6), by_tile(down), factor)
    factor = jnp.where(in_range(lane, 12, 6), by_tile(sec), factor)
    factor = jnp.where(in_range(lane, RIGHT, 4), -right, factor)
    factor = jnp.where(pull, jnp.where(even, -2.0, 2.0) * right, factor)
    shift = [offset[0, 0, 0, d, 0].astype(F32) for d in range(2)]
    moved = (~even) & ((lane < 6) | pull)
    lines = [factor]
    lines += [jnp.where(moved, shift[d], 0.0) for d in range(2)]
    lines += [by_tile([stiff[0, 0, t] for t in range(2)])]
    lines += [jnp.full((8, LANES), shift[d], F32) for d in range(2)]
    total = jnp.zeros((8, LANES), F32)
    for n, line in enumerate(lines):
        total = jnp.where(row == n, line, total)
    facts[...] = total


def pair_moments(kind, strips, sent, second, grad, misfit, pad):
    for t in range(2):
        rows = pl.ds(H * t, H)
        store_gradients(
            lambda lt: sent[rows, lt * LANES : (lt + 1) * LANES].astype(F32), grad.at[t, 0], grad.at[t, 1], pad
        )
        misfit[t] = sent[rows, :].astype(F32) - strips[0, 0, t, (2, 4)[kind]].astype(F32)
    sums = {}
    for lt in range(4):
        lanes = pl.ds(lt * LANES, LANES)
        cross, pull = {}, {}
        for t in range(2):
            g = [grad.at[t, 0], grad.at[t, 1], second.at[kind, t, 0], second.at[kind, t, 1]]
            got = accumulate(pair_fields(*g, misfit.at[t], lanes), PAIR_LEVEL)
            for n in range(4):
                cross[(n, t)] = got[n]
                pull[(n, t)] = got[4 + n]
        put_group(0, lt, cross, sums)
        put_group(1, lt, pull, sums)
    return sums


def sec_kernel(strips, before, second, out, grad, misfit, pad):
    sums = pair_moments(1, strips, before, second, grad, misfit, pad)
    for m in range(6):
        for group in range(2):
            out[m, pl.ds(8 * group, 8)] = sums.get((m, group), jnp.zeros((8, LANES), F32))


def down_kernel(strips, upper, before, second, own, facts, sec, out, grad, misfit, pad, table, wide):
    sums = pair_moments(0, strips, upper, second, grad, misfit, pad)
    for m in range(6):
        sums[(m, 2)] = sums.get((m, 1), jnp.zeros((8, LANES), F32))
        sums[(m, 1)] = sec[m, 0:8]
        sums[(m, 3)] = sec[m, 8:16]
    moments = own[...] + column_moments(sums, 4, table, wide, CROSS[0])
    lane = iota((1, LANES), 1)
    wide_lane = iota((8, LANES), 1)
    factor, au, av = facts[0:1, :], facts[1:2, :], facts[2:3, :]
    told = []
    for kind, sent in enumerate((upper, before)):
        known = sent[2 * H :, 0:LANES].astype(F32)
        exists, dx, dy = known[0:1], known[1:2], known[2:3]
        told += [dx, dy]
        alone = in_range(lane, (18, AGAIN)[kind], 6)
        pull_b = in_range(lane, PULL[kind] + 4, 4)
        factor = jnp.where(alone, exists, factor)
        factor = jnp.where(in_range(lane, CROSS[kind], 8), -exists, factor)
        factor = jnp.where(in_range(lane, PULL[kind], 4), -2.0 * exists, factor)
        factor = jnp.where(pull_b, 2.0 * exists, factor)
        au = jnp.where(alone | pull_b, dx, au)
        av = jnp.where(alone | pull_b, dy, av)
    au = au * (1.0 / W)
    av = av * (1.0 / H)
    one, u, v, uu, uv, vv = (moments[n : n + 1, :] for n in range(6))
    lines = [one, u + au * one, v + av * one, uu + 2.0 * au * u + au * au * one,
             uv + au * v + av * u + au * av * one, vv + 2.0 * av * v + av * av * one]
    row = iota((8, LANES), 0)
    full = jnp.zeros((8, LANES), F32)
    for n, line in enumerate(lines):
        full = jnp.where(row == n, line * factor, full)

    def back(x, by):
        return pltpu.roll(x, LANES - by, 1)

    alone = functools.reduce(jnp.add, [pltpu.roll(full, by, 1) for by in (58, 52, 46, 40, LANES + 58 - AGAIN)])
    ends = in_range(wide_lane, 58, 2) | in_range(wide_lane, 62, 2)
    alone = jnp.where(ends & ((row == 0) | (row == 3) | (row == 5)), alone + facts[3:4, :], alone)
    load = full + back(full, 24) + back(full, 32)
    final = jnp.where(in_range(wide_lane, 28, 4), load, full)
    final = jnp.where(in_range(wide_lane, 52, 4), back(full, 4), final)
    final = jnp.where(in_range(wide_lane, 58, 6), alone, final)
    tail = (told, [facts[4:5, :], facts[5:6, :]])
    for r in range(2):
        line = jnp.zeros((1, LANES), F32)
        for n, value in enumerate(tail[r]):
            line = jnp.where(in_range(lane, 120 + 2 * n, 2), value, line)
        for n, move in ((2, 56), (1, 16), (0, 104)):
            part = pltpu.roll(final, move, 1)[3 * r + n : 3 * r + n + 1, :]
            line = jnp.where(in_range(lane, 40 * n, 40), part, line)
        out[r : r + 1, :] = line


def solve_kernel(mine, theirs, update_out, residual_out, table):
    core = lax.axis_index("core")
    place = lax.axis_index("y") * 32 + lax.axis_index("tile")
    sub = iota((8, LANES), 0)
    lane = iota((8, LANES), 1)
    c0 = (sub & 1) == 0
    t0 = (sub & 2) == 0
    live = sub < 4
    for r in range(2):
        a = mine[pl.ds(r, LANES, stride=2), :]
        b = theirs[pl.ds(r, LANES, stride=2), :]
        first = jnp.where(core == 0, a, b)
        second = jnp.where(core == 0, b, a)
        table[pl.ds(256 * r, LANES, stride=2), :] = first.T
        table[pl.ds(256 * r + 1, LANES, stride=2), :] = second.T

    def read(r, place):
        return table[pl.ds(256 * r + 4 * place, 8), :]

    def low3(place):
        return read(0, 20 + place), read(0, 40 + place), read(0, place)

    def all6(place):
        return (read(1, place), read(1, 20 + place), read(0, 20 + place), read(1, 40 + place),
                read(0, 40 + place), read(0, place))

    def swap_tile(x):
        return jnp.where(t0, pltpu.roll(x, 6, 0), pltpu.roll(x, 2, 0))

    def swap_core(x):
        return jnp.where(c0, pltpu.roll(x, 7, 0), pltpu.roll(x, 1, 0))

    def row_from_next(x):
        return pltpu.roll(x, LANES - 1, 1)

    def row_to_next(x):
        return pltpu.roll(x, 1, 1)

    def sec_from_next(x):
        x = swap_core(x)
        return jnp.where(c0, x, pltpu.roll(x, LANES - 32, 1))

    def sec_to_next(x):
        x = swap_core(x)
        return jnp.where(c0, pltpu.roll(x, 32, 1), x)

    zero = jnp.zeros((8, LANES), F32)
    du = [read(1, 60) * (1.0 / W), read(0, 60) * (1.0 / W), read(0, 62) * (1.0 / W)]
    dv = [read(1, 61) * (1.0 / H), read(0, 61) * (1.0 / H), read(0, 63) * (1.0 / H)]
    au = jnp.where(t0, zero, du[0])
    av = jnp.where(t0, zero, dv[0])
    bu = jnp.where(t0, du[0], zero)
    bv = jnp.where(t0, dv[0], zero)
    blocks = [all6(17 + n) for n in range(3)]
    square = ((0, 1, 2), (1, 3, 4), (2, 4, 5))
    diagonal = [[blocks[(i // 3) + (j // 3)][square[i % 3][j % 3]] for j in range(6)] for i in range(6)]

    lower = [[None] * 6 for _ in range(6)]
    inverse_pivot = []
    work = {(i, j): diagonal[i][j] for i in range(6) for j in range(i + 1)}
    for j in range(6):
        inv = 1.0 / work[(j, j)]
        inverse_pivot.append(inv)
        for i in range(j + 1, 6):
            lower[i][j] = work[(i, j)] * inv
        for i in range(j + 1, 6):
            for k in range(j + 1, i + 1):
                work[(i, k)] = work[(i, k)] - lower[i][j] * work[(k, j)]
    inverse = [[None] * 6 for _ in range(6)]
    for j in range(6):
        for i in range(j + 1, 6):
            value = lower[i][j]
            for k in range(j + 1, i):
                value = value + lower[i][k] * inverse[k][j]
            inverse[i][j] = -value

    def precondition(v):
        mid = []
        for i in range(6):
            value = v[i]
            for j in range(i):
                value = value + inverse[i][j] * v[j]
            mid.append(value * inverse_pivot[i])
        out = []
        for i in range(6):
            value = mid[i]
            for j in range(i + 1, 6):
                value = value + inverse[j][i] * mid[j]
            out.append(value)
        return out

    def coupling(m, ra, rb, ca, cb):
        uu, uv, u, vv, v, one = m
        if ra is None:
            return [[uu + ca * u, uv + cb * u, u], [uv + ca * v, vv + cb * v, v], [u + ca * one, v + cb * one, one]]
        return [[uu + (ra + ca) * u, uv + ra * v + cb * u, u + ra * one],
                [uv + ca * v + rb * u, vv + (rb + cb) * v, v + rb * one],
                [u + ca * one, v + cb * one, one]]

    def join(xx, xy, yx, yy):
        return [a + b for a, b in zip(xx, xy)] + [a + b for a, b in zip(yx, yy)]

    down, across = (
        join(*(coupling(all6(place + i), None, None, du[n], dv[n]) for i in range(4))) for n, place in ((1, 4), (2, 8))
    )
    a6, b6 = all6(0), all6(1)
    sa6, sb6 = [swap_tile(x) for x in a6], [swap_tile(x) for x in b6]

    def pick(x, y):
        return [jnp.where(t0, p, q) for p, q in zip(x, y)]

    right = (pick(a6, sa6), pick(sa6, sb6), pick(b6, a6), pick(sb6, b6))
    right = join(*(coupling(m, au, av, bu, bv) for m in right))

    load = []
    for n in range(2):
        for x, y, z in zip(low3(2 + n), low3(12 + n), low3(14 + n)):
            load.append(x + row_from_next(y) + sec_from_next(z))

    def times(block, vector, transpose):
        out = []
        for i in range(6):
            value = None
            for j in range(6):
                term = (block[j][i] if transpose else block[i][j]) * vector[j]
                value = term if value is None else value + term
            out.append(value)
        return out

    down_next = [[row_from_next(x) for x in line] for line in down]
    across_next = [[sec_from_next(x) for x in line] for line in across]

    def multiply(vector):
        parts = [
            times(diagonal, vector, False),
            times(right, [swap_tile(x) for x in vector], False),
            times(down_next, [row_from_next(x) for x in vector], False),
            times(down, [row_to_next(x) for x in vector], True),
            times(across_next, [sec_from_next(x) for x in vector], False),
            times(across, [sec_to_next(x) for x in vector], True),
        ]
        return [functools.reduce(jnp.add, line) for line in zip(*parts)]

    def inner(x, y):
        total = functools.reduce(jnp.add, [a * b for a, b in zip(x, y)])
        total = jnp.where(live, total, 0.0)
        return jnp.sum(total, axis=(0, 1), keepdims=True)

    residual = load
    for step in range(ITERS):
        scaled = precondition(residual)
        image = multiply(scaled)
        rho_next, energy = inner(residual, scaled), inner(scaled, image)
        if step == 0:
            direction, product = scaled, image
            size = rho_next / energy
            update = [size * d for d in direction]
        else:
            ratio = rho_next / rho
            size = rho_next / (energy - ratio * rho_next / size)
            direction = [z + ratio * d for z, d in zip(scaled, direction)]
            product = [z + ratio * d for z, d in zip(image, product)]
            update = [x + size * d for x, d in zip(update, direction)]
        residual = [r - size * p for r, p in zip(residual, product)]
        rho = rho_next

    here = (lane == place) & live & ((sub & 1) == core)
    for vector, out in ((update, update_out), (residual, residual_out)):
        found = zero
        for i in range(6):
            value = jnp.sum(jnp.where(here, vector[i], 0.0), axis=1, keepdims=True)
            found = jnp.where(lane == i, value, found)
        found = found + pltpu.roll(found, 7, 0)
        out[0, 0, 0:1] = found[0:1, :6]
        out[0, 0, 1:2] = found[2:3, :6]


def shards(tile_strips, pair_mask, strip_offset, stiffness):
    tiles = lax.axis_size("tile")
    chips = lax.axis_size("y") * tiles
    sections = lax.axis_size("y") * 2
    offset = jnp.swapaxes(strip_offset, 3, 4)
    image = jax.ShapeDtypeStruct((ROWS, W), tile_strips.dtype)
    bottoms, patches = pl.pallas_call(
        pack_kernel,
        out_shape=(image, image),
        in_specs=[pl.BlockSpec(memory_space=pltpu.HBM)] * 3,
        out_specs=(VMEM, VMEM),
        scratch_shapes=[pltpu.SMEM(pair_mask.shape, jnp.int32), pltpu.SMEM(offset.shape, jnp.int32),
                        pltpu.SemaphoreType.DMA((4,)), pltpu.SemaphoreType.DMA((2,))],
        cost_estimate=pl.CostEstimate(flops=0, bytes_accessed=0, transcendentals=0),
        compiler_params=pltpu.CompilerParams(vmem_limit_bytes=PACK_LIMIT),
        name="pack",
    )(*(pltpu.with_memory_space_constraint(x, pltpu.HBM) for x in (tile_strips, pair_mask, offset)))
    upper = lax.ppermute(bottoms, "tile", [(i, (i + 1) % tiles) for i in range(tiles)])
    before = lax.ppermute(patches, ("y", "core"), [(i, (i + 1) % sections) for i in range(sections)])
    small = jax.ShapeDtypeStruct((8, LANES), F32)
    wide = pltpu.VMEM((8, LANES), F32)
    pad = pltpu.VMEM((4, H + 16, LANES), F32)
    params = pltpu.CompilerParams(vmem_limit_bytes=6 << 20)
    own, facts, second = pl.pallas_call(
        own_kernel,
        out_shape=(small, small, jax.ShapeDtypeStruct((2, 2, 2, H, W), F32)),
        in_specs=[VMEM, SMEM, SMEM, SMEM],
        out_specs=(VMEM, VMEM, VMEM),
        scratch_shapes=[pltpu.VMEM((2, 2, 2, H, W), F32), pltpu.VMEM((H, W), F32), pltpu.VMEM((6, 32, LANES), F32), wide, pad],
        cost_estimate=pl.CostEstimate(flops=20_000_000, bytes_accessed=700_000, transcendentals=0),
        compiler_params=params,
        name="own_moments",
    )(tile_strips, pair_mask, offset, stiffness)
    scratch = [pltpu.VMEM((2, 2, H, W), F32), pltpu.VMEM((2, H, W), F32), pad]
    cost = pl.CostEstimate(flops=10_000_000, bytes_accessed=900_000, transcendentals=0)
    sec = pl.pallas_call(
        sec_kernel,
        out_shape=jax.ShapeDtypeStruct((6, 16, LANES), F32),
        in_specs=[VMEM] * 3,
        out_specs=VMEM,
        scratch_shapes=scratch,
        cost_estimate=cost,
        compiler_params=params,
        name="sec_moments",
    )(tile_strips, before, second)
    message = pl.pallas_call(
        down_kernel,
        out_shape=jax.ShapeDtypeStruct((2, LANES), F32),
        in_specs=[VMEM] * 7,
        out_specs=VMEM,
        scratch_shapes=[*scratch, pltpu.VMEM((6, 32, LANES), F32), wide],
        cost_estimate=cost,
        compiler_params=params,
        name="down_moments",
    )(tile_strips, upper, before, second, own, facts, sec)
    sent = jnp.broadcast_to(message[None], (chips, 2, LANES))
    mine = lax.all_to_all(sent, ("y", "tile"), 0, 0)
    theirs = lax.ppermute(mine, "core", [(0, 1), (1, 0)])
    out = jax.ShapeDtypeStruct((1, 1, 2, 6), F32)
    outs = pl.pallas_call(
        solve_kernel,
        out_shape=(out, out),
        in_specs=[VMEM] * 2,
        out_specs=(VMEM, VMEM),
        scratch_shapes=[pltpu.VMEM((2 * 256 + 8, LANES), F32)],
        compiler_params=pltpu.CompilerParams(vmem_limit_bytes=4 << 20),
        name="solve",
    )(mine.reshape(chips * 2, LANES), theirs.reshape(chips * 2, LANES))
    return tuple(jnp.transpose(x, (3, 0, 1, 2)) for x in outs)


def solution(mesh):
    fine = Mesh(mesh.devices.reshape(4, 2, 32), ("y", "core", "tile"))
    sec = ("y", "core")
    return jax.shard_map(
        shards,
        mesh=fine,
        in_specs=(
            P(sec, "tile", None, None, None, None),
            P(sec, "tile", None, None),
            P(sec, "tile", None, None, None),
            P(sec, "tile", None),
        ),
        out_specs=(P(None, sec, "tile", None), P(None, sec, "tile", None)),
        check_vma=False,
    )
```

```python
import functools

import jax
import jax.numpy as jnp
from jax import lax
from jax.experimental import pallas as pl
from jax.experimental.pallas import tpu as pltpu
from jax.sharding import Mesh, PartitionSpec as P


ITERS = 3
H, W = 64, 512
F32 = jnp.float32
LANES = 128
RIGHT, CROSS, PULL, AGAIN = 24, (32, 40), (48, 56), 64
ROWS = 2 * H + 8
SCALE = 2.0**-17

PACK_LIMIT = 2 << 20

VMEM = pl.BlockSpec(memory_space=pltpu.VMEM)
SMEM = pl.BlockSpec(memory_space=pltpu.SMEM)


def iota(shape, axis):
    return lax.broadcasted_iota(jnp.int32, shape, axis)


def store_gradients(image, gx_ref, gy_ref, pad):
    lane = iota((8, LANES), 1)
    inner_first, inner_last = lane > 0, lane < LANES - 1
    zero = jnp.zeros((8, LANES), F32)
    tiles = []
    for lt in range(4):
        x = image(lt)
        pad[lt, 0:8] = zero
        pad[lt, 8 : 8 + H] = x
        pad[lt, 8 + H : 16 + H] = zero
        tiles.append([x[8 * k : 8 * k + 8] for k in range(8)])
    for k in range(8):
        ahead = [pltpu.roll(tiles[lt][k], LANES - 1, 1) for lt in range(4)] + [zero]
        behind = [zero] + [pltpu.roll(tiles[lt][k], 1, 1) for lt in range(4)]
        for lt in range(4):
            here = pl.ds(8 * k, 8), pl.ds(lt * LANES, LANES)
            gx_ref[here] = jnp.where(inner_last, ahead[lt], ahead[lt + 1]) - jnp.where(
                inner_first, behind[lt + 1], behind[lt]
            )
            gy_ref[here] = pad[lt, 9 + 8 * k : 17 + 8 * k] - pad[lt, 7 + 8 * k : 15 + 8 * k]


def row_moments(sums, level):
    c = 0.5 + iota((8, LANES), 0).astype(F32) / H
    out = [sums[0], c * sums[0] - sums[1] * 0.125]
    if level == 3:
        out.append((c * c) * sums[0] - (0.25 * c + 1.0 / 64.0) * sums[1] + sums[2] * (1.0 / 32.0))
    return out


def accumulate(fields, level):
    sums = None
    for k in range(8):
        values = fields(k)
        if sums is None:
            sums = [[v] * lv for v, lv in zip(values, level)]
            continue
        new = []
        for v, old, lv in zip(values, sums, level):
            now = [old[0] + v]
            for q in range(1, lv):
                now.append(old[q] + now[q - 1])
            new.append(now)
        sums = new
    return [row_moments(s, lv) for s, lv in zip(sums, level)]


def tree8(vs):
    s = iota((8, LANES), 0)
    m4 = s < 4
    w = []
    for i in range(4):
        x = jnp.where(m4, vs[i], vs[i + 4])
        y = jnp.where(m4, vs[i + 4], vs[i])
        w.append(x + pltpu.roll(y, 4, 0))
    m2 = (s & 2) == 0
    z = []
    for i in range(2):
        x = jnp.where(m2, w[i], w[i + 2])
        y = jnp.where(m2, w[i + 2], w[i])
        z.append(x + jnp.where(m2, pltpu.roll(y, 6, 0), pltpu.roll(y, 2, 0)))
    m1 = (s & 1) == 0
    x = jnp.where(m1, z[0], z[1])
    y = jnp.where(m1, z[1], z[0])
    return x + jnp.where(m1, pltpu.roll(y, 7, 0), pltpu.roll(y, 1, 0))


def put_group(group, lt, found, total):
    order = [found[(f, t)] for f in range(4) for t in range(2)]
    low = [tree8([v[q] for v in order]) for q in range(2)]
    u = (iota((8, LANES), 1) + lt * LANES).astype(F32) / W - 0.5
    new = [low[0], u * low[0], low[1]]
    if any(len(v) > 2 for v in order):
        zero = jnp.zeros((8, LANES), F32)
        new += [(u * u) * low[0], u * low[1], tree8([v[2] if len(v) > 2 else zero for v in order])]
    for m, value in enumerate(new):
        total[(m, group)] = total[(m, group)] + value if lt else value


def column_moments(total, groups, table, wide, start=0):
    dims = (((1,), (1,)), ((), ()))
    zero = jnp.zeros((8, LANES), F32)
    scale = jnp.full((8, LANES), SCALE, F32)
    row = iota((8, 8 * groups), 0)
    out = None
    for m in range(6):
        for group in range(groups):
            table[m, pl.ds(8 * group, 8)] = total.get((m, group), zero)
        part = lax.dot_general(
            scale, table[m], dims, precision=lax.Precision.HIGHEST, preferred_element_type=F32
        )
        out = part if out is None else jnp.where(row == m, part, out)
    wide[...] = zero
    wide[0:6, start : start + 8 * groups] = out[0:6]
    return wide[...]


def pair_fields(gxa, gya, gxb, gyb, misfit, lanes):
    def fields(k):
        rows = pl.ds(8 * k, 8)
        xa, ya, xb, yb, m = (ref[rows, lanes] for ref in (gxa, gya, gxb, gyb, misfit))
        return [xa * xb, xa * yb, ya * xb, ya * yb, xa * m, ya * m, xb * m, yb * m]

    return fields


def self_fields(gx, gy, lanes):
    def fields(k):
        rows = pl.ds(8 * k, 8)
        x, y = gx[rows, lanes], gy[rows, lanes]
        return [x * x, x * y, y * y]

    return fields


PAIR_LEVEL = (3, 3, 3, 3, 2, 2, 2, 2)


def by_tile(values, shape=(8, LANES)):
    return jnp.where((iota(shape, 1) & 1) == 0, values[0], values[1])


def in_range(lane, start, length):
    return (lane >= start) & (lane < start + length)


def own_exists(mask):
    down = lax.axis_index("tile") < 31
    sec = 2 * lax.axis_index("y") + lax.axis_index("core") < 7
    out = []
    for k, inside in ((1, down), (2, sec)):
        out.append([jnp.where((mask[0, 0, t, k] == 1) & inside, 1.0, 0.0) for t in range(2)])
    return out


def pack_kernel(strips, mask_in, offset_in, bottoms, patches, mask, offset, sems, small_sems):
    small = [pltpu.make_async_copy(mask_in, mask, small_sems.at[0]),
             pltpu.make_async_copy(offset_in, offset, small_sems.at[1])]
    for copy in small:
        copy.start()
    copies = []
    for n, (ref, image) in enumerate(((bottoms, 3), (patches, 4))):
        for t in range(2):
            copies.append(
                pltpu.make_async_copy(strips.at[0, 0, t, image], ref.at[pl.ds(H * t, H)], sems.at[2 * n + t])
            )
    for copy in copies:
        copy.start()
    for copy in small:
        copy.wait()
    exists = own_exists(mask)
    row = iota((8, W), 0)
    for n, ref in enumerate((bottoms, patches)):
        lines = [by_tile(exists[n], (8, W))]
        for d in range(2):
            lines.append(by_tile([offset[0, 0, t, d, n + 1].astype(F32) for t in range(2)], (8, W)))
        block = jnp.where(row == 0, lines[0], jnp.where(row == 1, lines[1], jnp.where(row == 2, lines[2], 0.0)))
        ref[2 * H :, :] = block.astype(jnp.bfloat16)
    for copy in copies:
        copy.wait()


def own_kernel(strips, mask, offset, stiff, out, facts, second, grad, misfit, table, wide, pad):
    kinds = ((1, 0), (3, 3), (4, 4), (2, 2))
    refs = {}
    for kind, images in enumerate(kinds):
        for t in range(2):
            home = grad.at[kind, t] if kind < 2 else second.at[3 - kind, t]
            refs[(kind, t)] = (home.at[0], home.at[1])
            store_gradients(
                lambda lt: strips[0, 0, t, images[t], :, lt * LANES : (lt + 1) * LANES].astype(F32), *refs[(kind, t)], pad
            )
    misfit[...] = strips[0, 0, 0, 1].astype(F32) - strips[0, 0, 1, 0].astype(F32)
    sums = {}
    for lt in range(4):
        lanes = pl.ds(lt * LANES, LANES)
        found = {}
        for kind in range(4):
            for t in range(2):
                got = accumulate(self_fields(*refs[(kind, t)], lanes), (3, 3, 3))
                for n in range(3):
                    found[(3 * kind + n, t)] = got[n]
        for group in range(3):
            put_group(group, lt, {(f, t): found[(4 * group + f, t)] for f in range(4) for t in range(2)}, sums)
        got = accumulate(pair_fields(*refs[(0, 0)], *refs[(0, 1)], misfit, lanes), PAIR_LEVEL)
        right = {(0, 0): got[0], (0, 1): got[1], (1, 0): got[2], (1, 1): got[3],
                 (2, 0): got[4], (3, 0): got[5], (2, 1): got[6], (3, 1): got[7]}
        put_group(3, lt, right, sums)
    found = column_moments(sums, 4, table, wide)
    row = iota((8, LANES), 0)
    lane = iota((8, LANES), 1)
    out[...] = found + jnp.where(in_range(lane, AGAIN, 6), pltpu.roll(found, AGAIN - 12, 1), 0.0)
    even = (lane & 1) == 0
    down, sec = own_exists(mask)
    right = jnp.where(mask[0, 0, 0, 0] == 1, 1.0, 0.0)
    pull = in_range(lane, RIGHT + 4, 4)
    factor = jnp.where(lane < 6, right, 0.0)
    factor = jnp.where(in_range(lane, 6, 6), by_tile(down), factor)
    factor = jnp.where(in_range(lane, 12, 6), by_tile(sec), factor)
    factor = jnp.where(in_range(lane, RIGHT, 4), -right, factor)
    factor = jnp.where(pull, jnp.where(even, -2.0, 2.0) * right, factor)
    shift = [offset[0, 0, 0, d, 0].astype(F32) for d in range(2)]
    moved = (~even) & ((lane < 6) | pull)
    lines = [factor]
    lines += [jnp.where(moved, shift[d], 0.0) for d in range(2)]
    lines += [by_tile([stiff[0, 0, t] for t in range(2)])]
    lines += [jnp.full((8, LANES), shift[d], F32) for d in range(2)]
    total = jnp.zeros((8, LANES), F32)
    for n, line in enumerate(lines):
        total = jnp.where(row == n, line, total)
    facts[...] = total


def pair_moments(kind, strips, sent, second, grad, misfit, pad):
    for t in range(2):
        rows = pl.ds(H * t, H)
        store_gradients(
            lambda lt: sent[rows, lt * LANES : (lt + 1) * LANES].astype(F32), grad.at[t, 0], grad.at[t, 1], pad
        )
        misfit[t] = sent[rows, :].astype(F32) - strips[0, 0, t, (2, 4)[kind]].astype(F32)
    sums = {}
    for lt in range(4):
        lanes = pl.ds(lt * LANES, LANES)
        cross, pull = {}, {}
        for t in range(2):
            g = [grad.at[t, 0], grad.at[t, 1], second.at[kind, t, 0], second.at[kind, t, 1]]
            got = accumulate(pair_fields(*g, misfit.at[t], lanes), PAIR_LEVEL)
            for n in range(4):
                cross[(n, t)] = got[n]
                pull[(n, t)] = got[4 + n]
        put_group(0, lt, cross, sums)
        put_group(1, lt, pull, sums)
    return sums


def sec_kernel(strips, before, second, out, grad, misfit, pad):
    sums = pair_moments(1, strips, before, second, grad, misfit, pad)
    for m in range(6):
        for group in range(2):
            out[m, pl.ds(8 * group, 8)] = sums.get((m, group), jnp.zeros((8, LANES), F32))


def down_kernel(strips, upper, before, second, own, facts, sec, out, grad, misfit, pad, table, wide):
    sums = pair_moments(0, strips, upper, second, grad, misfit, pad)
    for m in range(6):
        sums[(m, 2)] = sums.get((m, 1), jnp.zeros((8, LANES), F32))
        sums[(m, 1)] = sec[m, 0:8]
        sums[(m, 3)] = sec[m, 8:16]
    moments = own[...] + column_moments(sums, 4, table, wide, CROSS[0])
    lane = iota((1, LANES), 1)
    wide_lane = iota((8, LANES), 1)
    factor, au, av = facts[0:1, :], facts[1:2, :], facts[2:3, :]
    told = []
    for kind, sent in enumerate((upper, before)):
        known = sent[2 * H :, 0:LANES].astype(F32)
        exists, dx, dy = known[0:1], known[1:2], known[2:3]
        told += [dx, dy]
        alone = in_range(lane, (18, AGAIN)[kind], 6)
        pull_b = in_range(lane, PULL[kind] + 4, 4)
        factor = jnp.where(alone, exists, factor)
        factor = jnp.where(in_range(lane, CROSS[kind], 8), -exists, factor)
        factor = jnp.where(in_range(lane, PULL[kind], 4), -2.0 * exists, factor)
        factor = jnp.where(pull_b, 2.0 * exists, factor)
        au = jnp.where(alone | pull_b, dx, au)
        av = jnp.where(alone | pull_b, dy, av)
    au = au * (1.0 / W)
    av = av * (1.0 / H)
    one, u, v, uu, uv, vv = (moments[n : n + 1, :] for n in range(6))
    lines = [one, u + au * one, v + av * one, uu + 2.0 * au * u + au * au * one,
             uv + au * v + av * u + au * av * one, vv + 2.0 * av * v + av * av * one]
    row = iota((8, LANES), 0)
    full = jnp.zeros((8, LANES), F32)
    for n, line in enumerate(lines):
        full = jnp.where(row == n, line * factor, full)

    def back(x, by):
        return pltpu.roll(x, LANES - by, 1)

    alone = functools.reduce(jnp.add, [pltpu.roll(full, by, 1) for by in (58, 52, 46, 40, LANES + 58 - AGAIN)])
    ends = in_range(wide_lane, 58, 2) | in_range(wide_lane, 62, 2)
    alone = jnp.where(ends & ((row == 0) | (row == 3) | (row == 5)), alone + facts[3:4, :], alone)
    load = full + back(full, 24) + back(full, 32)
    final = jnp.where(in_range(wide_lane, 28, 4), load, full)
    final = jnp.where(in_range(wide_lane, 52, 4), back(full, 4), final)
    final = jnp.where(in_range(wide_lane, 58, 6), alone, final)
    tail = (told, [facts[4:5, :], facts[5:6, :]])
    for r in range(2):
        line = jnp.zeros((1, LANES), F32)
        for n, value in enumerate(tail[r]):
            line = jnp.where(in_range(lane, 120 + 2 * n, 2), value, line)
        for n, move in ((2, 56), (1, 16), (0, 104)):
            part = pltpu.roll(final, move, 1)[3 * r + n : 3 * r + n + 1, :]
            line = jnp.where(in_range(lane, 40 * n, 40), part, line)
        out[r : r + 1, :] = line


def solve_kernel(mine, theirs, update_out, residual_out, table):
    core = lax.axis_index("core")
    place = lax.axis_index("y") * 32 + lax.axis_index("tile")
    sub = iota((8, LANES), 0)
    lane = iota((8, LANES), 1)
    c0 = (sub & 1) == 0
    t0 = (sub & 2) == 0
    live = sub < 4
    for r in range(2):
        a = mine[pl.ds(r, LANES, stride=2), :]
        b = theirs[pl.ds(r, LANES, stride=2), :]
        table[pl.ds(256 * r + core, LANES, stride=2), :] = a.T
        table[pl.ds(256 * r + 1 - core, LANES, stride=2), :] = b.T

    def read(r, place):
        return table[pl.ds(256 * r + 4 * place, 8), :]

    def low3(place):
        return read(0, 20 + place), read(0, 40 + place), read(0, place)

    def all6(place):
        return (read(1, place), read(1, 20 + place), read(0, 20 + place), read(1, 40 + place),
                read(0, 40 + place), read(0, place))

    def swap_tile(x):
        return jnp.where(t0, pltpu.roll(x, 6, 0), pltpu.roll(x, 2, 0))

    def swap_core(x):
        return jnp.where(c0, pltpu.roll(x, 7, 0), pltpu.roll(x, 1, 0))

    def row_from_next(x):
        return pltpu.roll(x, LANES - 1, 1)

    def row_to_next(x):
        return pltpu.roll(x, 1, 1)

    def sec_from_next(x):
        x = swap_core(x)
        return jnp.where(c0, x, pltpu.roll(x, LANES - 32, 1))

    def sec_to_next(x):
        x = swap_core(x)
        return jnp.where(c0, pltpu.roll(x, 32, 1), x)

    zero = jnp.zeros((8, LANES), F32)
    du = [read(1, 60) * (1.0 / W), read(0, 60) * (1.0 / W), read(0, 62) * (1.0 / W)]
    dv = [read(1, 61) * (1.0 / H), read(0, 61) * (1.0 / H), read(0, 63) * (1.0 / H)]
    au = jnp.where(t0, zero, du[0])
    av = jnp.where(t0, zero, dv[0])
    bu = jnp.where(t0, du[0], zero)
    bv = jnp.where(t0, dv[0], zero)
    blocks = [all6(17 + n) for n in range(3)]
    square = ((0, 1, 2), (1, 3, 4), (2, 4, 5))
    diagonal = [[blocks[(i // 3) + (j // 3)][square[i % 3][j % 3]] for j in range(6)] for i in range(6)]

    lower = [[None] * 6 for _ in range(6)]
    inverse_pivot = []
    work = {(i, j): diagonal[i][j] for i in range(6) for j in range(i + 1)}
    for j in range(6):
        inv = 1.0 / work[(j, j)]
        inverse_pivot.append(inv)
        for i in range(j + 1, 6):
            lower[i][j] = work[(i, j)] * inv
        for i in range(j + 1, 6):
            for k in range(j + 1, i + 1):
                work[(i, k)] = work[(i, k)] - lower[i][j] * work[(k, j)]
    inverse = [[None] * 6 for _ in range(6)]
    for j in range(6):
        for i in range(j + 1, 6):
            value = lower[i][j]
            for k in range(j + 1, i):
                value = value + lower[i][k] * inverse[k][j]
            inverse[i][j] = -value

    def precondition(v):
        mid = []
        for i in range(6):
            value = v[i]
            for j in range(i):
                value = value + inverse[i][j] * v[j]
            mid.append(value * inverse_pivot[i])
        out = []
        for i in range(6):
            value = mid[i]
            for j in range(i + 1, 6):
                value = value + inverse[j][i] * mid[j]
            out.append(value)
        return out

    def coupling(m, ra, rb, ca, cb):
        uu, uv, u, vv, v, one = m
        if ra is None:
            return [[uu + ca * u, uv + cb * u, u], [uv + ca * v, vv + cb * v, v], [u + ca * one, v + cb * one, one]]
        return [[uu + (ra + ca) * u, uv + ra * v + cb * u, u + ra * one],
                [uv + ca * v + rb * u, vv + (rb + cb) * v, v + rb * one],
                [u + ca * one, v + cb * one, one]]

    def join(xx, xy, yx, yy):
        return [a + b for a, b in zip(xx, xy)] + [a + b for a, b in zip(yx, yy)]

    down, across = (
        join(*(coupling(all6(place + i), None, None, du[n], dv[n]) for i in range(4))) for n, place in ((1, 4), (2, 8))
    )
    a6, b6 = all6(0), all6(1)
    sa6, sb6 = [swap_tile(x) for x in a6], [swap_tile(x) for x in b6]

    def pick(x, y):
        return [jnp.where(t0, p, q) for p, q in zip(x, y)]

    right = (pick(a6, sa6), pick(sa6, sb6), pick(b6, a6), pick(sb6, b6))
    right = join(*(coupling(m, au, av, bu, bv) for m in right))

    load = []
    for n in range(2):
        for x, y, z in zip(low3(2 + n), low3(12 + n), low3(14 + n)):
            load.append(x + row_from_next(y) + sec_from_next(z))

    def times(block, vector, transpose):
        out = []
        for i in range(6):
            value = None
            for j in range(6):
                term = (block[j][i] if transpose else block[i][j]) * vector[j]
                value = term if value is None else value + term
            out.append(value)
        return out

    down_next = [[row_from_next(x) for x in line] for line in down]
    across_next = [[sec_from_next(x) for x in line] for line in across]

    def multiply(vector):
        parts = [
            times(diagonal, vector, False),
            times(right, [swap_tile(x) for x in vector], False),
            times(down_next, [row_from_next(x) for x in vector], False),
            times(down, [row_to_next(x) for x in vector], True),
            times(across_next, [sec_from_next(x) for x in vector], False),
            times(across, [sec_to_next(x) for x in vector], True),
        ]
        return [functools.reduce(jnp.add, line) for line in zip(*parts)]

    def inner(x, y):
        total = functools.reduce(jnp.add, [a * b for a, b in zip(x, y)])
        total = jnp.where(live, total, 0.0)
        return jnp.sum(total, axis=(0, 1), keepdims=True)

    residual = load
    for step in range(ITERS):
        scaled = precondition(residual)
        image = multiply(scaled)
        rho_next, energy = inner(residual, scaled), inner(scaled, image)
        if step == 0:
            direction, product = scaled, image
            size = rho_next / energy
            update = [size * d for d in direction]
        else:
            ratio = rho_next / rho
            size = rho_next / (energy - ratio * rho_next / size)
            direction = [z + ratio * d for z, d in zip(scaled, direction)]
            product = [z + ratio * d for z, d in zip(image, product)]
            update = [x + size * d for x, d in zip(update, direction)]
        residual = [r - size * p for r, p in zip(residual, product)]
        rho = rho_next

    here = (lane == place) & live & ((sub & 1) == core)
    for vector, out in ((update, update_out), (residual, residual_out)):
        found = zero
        for i in range(6):
            value = jnp.sum(jnp.where(here, vector[i], 0.0), axis=1, keepdims=True)
            found = jnp.where(lane == i, value, found)
        found = found + pltpu.roll(found, 7, 0)
        out[0, 0, 0:1] = found[0:1, :6]
        out[0, 0, 1:2] = found[2:3, :6]


def shards(tile_strips, pair_mask, strip_offset, stiffness):
    tiles = lax.axis_size("tile")
    chips = lax.axis_size("y") * tiles
    sections = lax.axis_size("y") * 2
    offset = jnp.swapaxes(strip_offset, 3, 4)
    image = jax.ShapeDtypeStruct((ROWS, W), tile_strips.dtype)
    bottoms, patches = pl.pallas_call(
        pack_kernel,
        out_shape=(image, image),
        in_specs=[pl.BlockSpec(memory_space=pltpu.HBM)] * 3,
        out_specs=(VMEM, VMEM),
        scratch_shapes=[pltpu.SMEM(pair_mask.shape, jnp.int32), pltpu.SMEM(offset.shape, jnp.int32),
                        pltpu.SemaphoreType.DMA((4,)), pltpu.SemaphoreType.DMA((2,))],
        cost_estimate=pl.CostEstimate(flops=0, bytes_accessed=0, transcendentals=0),
        compiler_params=pltpu.CompilerParams(vmem_limit_bytes=PACK_LIMIT),
        name="pack",
    )(*(pltpu.with_memory_space_constraint(x, pltpu.HBM) for x in (tile_strips, pair_mask, offset)))
    upper = lax.ppermute(bottoms, "tile", [(i, (i + 1) % tiles) for i in range(tiles)])
    before = lax.ppermute(patches, ("y", "core"), [(i, (i + 1) % sections) for i in range(sections)])
    small = jax.ShapeDtypeStruct((8, LANES), F32)
    wide = pltpu.VMEM((8, LANES), F32)
    pad = pltpu.VMEM((4, H + 16, LANES), F32)
    params = pltpu.CompilerParams(vmem_limit_bytes=6 << 20)
    own, facts, second = pl.pallas_call(
        own_kernel,
        out_shape=(small, small, jax.ShapeDtypeStruct((2, 2, 2, H, W), F32)),
        in_specs=[VMEM, SMEM, SMEM, SMEM],
        out_specs=(VMEM, VMEM, VMEM),
        scratch_shapes=[pltpu.VMEM((2, 2, 2, H, W), F32), pltpu.VMEM((H, W), F32), pltpu.VMEM((6, 32, LANES), F32), wide, pad],
        cost_estimate=pl.CostEstimate(flops=20_000_000, bytes_accessed=700_000, transcendentals=0),
        compiler_params=params,
        name="own_moments",
    )(tile_strips, pair_mask, offset, stiffness)
    scratch = [pltpu.VMEM((2, 2, H, W), F32), pltpu.VMEM((2, H, W), F32), pad]
    cost = pl.CostEstimate(flops=10_000_000, bytes_accessed=900_000, transcendentals=0)
    sec = pl.pallas_call(
        sec_kernel,
        out_shape=jax.ShapeDtypeStruct((6, 16, LANES), F32),
        in_specs=[VMEM] * 3,
        out_specs=VMEM,
        scratch_shapes=scratch,
        cost_estimate=cost,
        compiler_params=params,
        name="sec_moments",
    )(tile_strips, before, second)
    message = pl.pallas_call(
        down_kernel,
        out_shape=jax.ShapeDtypeStruct((2, LANES), F32),
        in_specs=[VMEM] * 7,
        out_specs=VMEM,
        scratch_shapes=[*scratch, pltpu.VMEM((6, 32, LANES), F32), wide],
        cost_estimate=cost,
        compiler_params=params,
        name="down_moments",
    )(tile_strips, upper, before, second, own, facts, sec)
    sent = jnp.broadcast_to(message[None], (chips, 2, LANES))
    mine = lax.all_to_all(sent, ("y", "tile"), 0, 0)
    theirs = lax.ppermute(mine, "core", [(0, 1), (1, 0)])
    out = jax.ShapeDtypeStruct((1, 1, 2, 6), F32)
    outs = pl.pallas_call(
        solve_kernel,
        out_shape=(out, out),
        in_specs=[VMEM] * 2,
        out_specs=(VMEM, VMEM),
        scratch_shapes=[pltpu.VMEM((2 * 256 + 8, LANES), F32)],
        compiler_params=pltpu.CompilerParams(vmem_limit_bytes=4 << 20),
        name="solve",
    )(mine.reshape(chips * 2, LANES), theirs.reshape(chips * 2, LANES))
    return tuple(jnp.transpose(x, (3, 0, 1, 2)) for x in outs)


def solution(mesh):
    fine = Mesh(mesh.devices.reshape(4, 2, 32), ("y", "core", "tile"))
    sec = ("y", "core")
    return jax.shard_map(
        shards,
        mesh=fine,
        in_specs=(
            P(sec, "tile", None, None, None, None),
            P(sec, "tile", None, None),
            P(sec, "tile", None, None, None),
            P(sec, "tile", None),
        ),
        out_specs=(P(None, sec, "tile", None), P(None, sec, "tile", None)),
        check_vma=False,
    )
```
